32 devices in a mesh: section: 4 (over z), tm: 8 (over y, x, core).
Axes of the slice: x: 2, y: 2, z: 4, core: 2. Of those that a mesh axis runs over, the one named last changes fastest.
Arguments:
- clean: float32 [4, 4, 512], P(None, None, 'tm'), may hold values from -6 to 6
- noise: float32 [4, 4, 512], P(None, None, 'tm'), may hold values from -6 to 6
- timestep: int32 [4], replicated, may hold values from 0 to 999
- lift: float32 [256], replicated, may hold values from -4 to 4
- norm_gain: float32 [4, 2, 256], P('section'), may hold values from 0.5 to 1.5
- norm_bias: float32 [4, 2, 256], P('section'), may hold values from -0.7 to 0.7
- conv_weight: bfloat16 [4, 2, 3, 3, 256, 256], P('section'), may hold values from -0.125 to 0.125
- time_proj: bfloat16 [4, 256, 256], P('section'), may hold values from -0.375 to 0.375
Outputs:
- skips: bfloat16 [4, 4, 4, 512, 256], P('section', None, None, 'tm')
The draws below stay inside these ranges and needn't reach their ends.
All inputs are finite; a program needn't handle non-finite values.
Results may differ from the reference program's by a relative error of at most 0.012.
Values may be sent and summed in bfloat16 or wider, within the bound.
A program may use at most 64 MiB of HBM per device.

```python
import math
import jax
import jax.numpy as jnp
from jax import lax

C = 256
GROUPS = 32
LAYERS = 2
MB = 4
FR = 4
STEPS = 1000
TD = 64
TIME = 512
N_SECTION = 4


def envelope(key):
    blocks = TIME // TD
    level_key, start_key = jax.random.split(jax.random.fold_in(key, 7001))
    log_level = jax.random.uniform(level_key, (MB, blocks), jnp.float32, -3.0, 1.5)
    run_length = min(3, blocks)
    run_start = jax.random.randint(start_key, (MB, 1), 0, blocks)
    positions = jnp.arange(blocks, dtype=jnp.int32)[None, :]
    silent = (positions - run_start) % blocks < run_length
    log_level = jnp.where(silent, -3.0, log_level)
    amplitude = jnp.exp(log_level)
    return jnp.repeat(amplitude, TD, axis=1)[:, None, :]


def draw_clean(key, part):
    amplitude = envelope(key)
    entry_key = jax.random.fold_in(key, 7002)
    entries = jax.random.normal(entry_key, (MB, FR, TIME), jnp.float32)
    return jnp.clip(entries * amplitude, -6.0, 6.0)


def draw_noise(key, part):
    amplitude = envelope(key)
    entry_key = jax.random.fold_in(key, 7003)
    entries = jax.random.normal(entry_key, (MB, FR, TIME), jnp.float32)
    return jnp.clip(entries * amplitude, -6.0, 6.0)


def touch_ends(drawn, stream_key, least, largest):
    spot = [jax.random.randint(jax.random.fold_in(stream_key, axis), (), 0, length) for axis, length in enumerate(drawn.shape)]
    main_axis = drawn.shape.index(max(drawn.shape))
    next_to = spot[:main_axis] + [(spot[main_axis] + 1) % drawn.shape[main_axis]] + spot[main_axis + 1:]
    return drawn.at[tuple(spot)].set(least).at[tuple(next_to)].set(largest)


def steps_of(rng, shape, shards, low, largest):
    factor_of = 1.0
    for dim, shards_of in shards:
        heights = jax.random.uniform(jax.random.fold_in(jax.random.fold_in(rng, 6), dim), (shards_of,), jnp.float32, low / len(shards), largest / len(shards))
        factor_of = factor_of * jnp.repeat(jnp.exp(heights), shape[dim] // shards_of).reshape((-1,) + (1,) * (len(shape) - 1 - dim))
    return factor_of


def normal_values(rng, extent, scale, bound, cuts=(), held_as=jnp.bfloat16):
    level = steps_of(rng, extent, cuts, -0.22, 0.18) if cuts else 1.0
    result = jax.random.normal(rng, extent, jnp.float32) * scale * level
    return jnp.minimum(jnp.maximum(result, -bound), bound).astype(held_as)


def setup_inputs(seed: int = 0) -> dict:
    splits = jax.random.split(jax.random.key(seed), 9)
    return {
        "clean": draw_clean(jax.random.fold_in(splits[8], 71), 0),
        "noise": draw_noise(jax.random.fold_in(splits[8], 71), 0),
        "timestep": touch_ends(jax.random.randint(splits[2], (MB,), 0, STEPS), jax.random.fold_in(splits[2], 1), 0, STEPS - 1).astype(jnp.int32),
        "lift": normal_values(splits[3], (C,), 1.0, 4.0, (), jnp.float32),
        "norm_gain": jnp.clip(1.0 + 0.1 * jax.random.normal(splits[4], (N_SECTION, LAYERS, C), jnp.float32), 0.5, 1.5),
        "norm_bias": jnp.clip(jax.random.uniform(splits[5], (N_SECTION, LAYERS, C), jnp.float32, -0.7, 0.7) * steps_of(splits[5], (N_SECTION, LAYERS, C), ((0, 4),), -0.4, 0.0), -0.7, 0.7),
        "conv_weight": normal_values(splits[6], (N_SECTION, LAYERS, 3, 3, C, C), (9 * C) ** -0.5, 0.125, ((0, 4),)),
        "time_proj": normal_values(splits[7], (N_SECTION, C, C), C ** -0.5, 0.375, ((0, 4),)),
    }


def prepare(clean, noise, timestep, lift):
    steps_f = timestep.astype(jnp.float32)
    level = jnp.cos(math.pi / 2.0 * (steps_f / STEPS + 0.008) / 1.008) ** 2
    noisy = jnp.sqrt(level)[:, None, None] * clean + jnp.sqrt(1.0 - level)[:, None, None] * noise
    lifted = (noisy[..., None] * lift).astype(jnp.bfloat16)
    half = C // 2
    freqs = jnp.exp(-math.log(10000.0) * jnp.arange(half, dtype=jnp.float32) / half)
    angles = steps_f[:, None] * freqs[None, :]
    emb = jnp.concatenate([jnp.sin(angles), jnp.cos(angles)], axis=1).astype(jnp.bfloat16)
    return (lifted, emb)

def group_act(h, gain, bias):
    rows_f, rows_t, width = h.shape
    grouped = h.reshape(rows_f, rows_t, GROUPS, width // GROUPS)
    count = rows_f * rows_t * (width // GROUPS)
    total = lax.optimization_barrier(jnp.sum(grouped, axis=(0, 1, 3)))
    square = lax.optimization_barrier(jnp.sum(grouped * grouped, axis=(0, 1, 3)))
    mean = total / count
    var = square / count - mean * mean
    inv = lax.rsqrt(var + 1e-05)
    normed = ((grouped - mean[:, None]) * inv[:, None]).reshape(h.shape) * gain + bias
    return jax.nn.silu(normed).astype(jnp.bfloat16)

def conv_same(padded, weight):
    rows_f = padded.shape[0]
    width_out = padded.shape[1] - 2
    chans = padded.shape[2]
    framed = jnp.pad(padded, ((1, 1), (0, 0), (0, 0)))
    total = jnp.zeros((rows_f * width_out, weight.shape[3]), jnp.float32)
    for i in range(3):
        for j in range(3):
            window = framed[i:i + rows_f, j:j + width_out].reshape(-1, chans)
            total = total + jnp.dot(window, weight[i, j], preferred_element_type=jnp.float32)
    return total.reshape(rows_f, width_out, weight.shape[3])

def reference(clean, noise, timestep, lift, norm_gain, norm_bias, conv_weight, time_proj):
    lifted, emb = prepare(clean, noise, timestep, lift)
    levels = []
    for section_id in range(N_SECTION):
        levels.append(jnp.dot(emb, time_proj[section_id], preferred_element_type=jnp.float32))
    results = []
    for micro in range(MB):
        current = lifted[micro]
        per_level = []
        for section_id in range(N_SECTION):
            depth = LAYERS if section_id < N_SECTION // 2 else 1
            hidden = current.astype(jnp.float32) + levels[section_id][micro]
            for layer in range(depth):
                act = group_act(hidden, norm_gain[section_id, layer], norm_bias[section_id, layer])
                padded = jnp.pad(act, ((0, 0), (1, 1), (0, 0)))
                hidden = hidden + conv_same(padded, conv_weight[section_id, layer])
            current = hidden.astype(jnp.bfloat16)
            per_level.append(current)
        results.append(jnp.stack(per_level))
    return jnp.stack(results, axis=1)
```

```python
import functools
import math

import jax
import jax.numpy as jnp
from jax import lax
from jax.experimental import pallas as pl
from jax.experimental.pallas import tpu as pltpu
from jax.sharding import PartitionSpec as P

GROUPS = 32
STEPS = 1000
MESH = pl.DeviceIdType.MESH


def silu(z):
    half = 0.5 * z
    return half + half * jnp.tanh(half)


def kernel(
    dims,
    steps_in,
    clean_in,
    noise_in,
    lift_in,
    gains_in,
    biases_in,
    proj_in,
    weights,
    staged,
    w,
    xin,
    hmid,
    heard,
    temb_next,
    spare_send,
    spare,
    clean,
    noise,
    lift,
    gains,
    biases,
    proj,
    noisy,
    temb,
    timestep,
    act3,
    st_send,
    st_recv,
    edge_send,
    edge_recv,
    st_ssem,
    st_rsem,
    edge_ssem,
    edge_rsem,
    blk_ssem,
    blk_rsem,
    w_sem,
    in_sem,
    heard_ssem,
    heard_rsem,
    temb_ssem,
    temb_rsem,
    spare_ssem,
    spare_rsem,
    part_ssem,
    part_rsem,
    share_ssem,
    share_rsem,
):
    n_time, n_section, micros, rows_f, frames, chans, layers, fuse = dims
    rows = rows_f * frames
    positions = rows * n_time
    width = chans // GROUPS
    count = positions * width
    sec = lax.axis_index("section")
    tm = lax.axis_index("tm")
    deep = sec < n_section // 2
    first = sec == 0
    last = sec == n_section - 1
    has_left = tm > 0
    has_right = tm < n_time - 1
    up = jnp.minimum(sec + 1, n_section - 1)
    down = jnp.maximum(sec - 1, 0)
    short = n_time <= 8
    taps = 9 * chans
    penult = sec == n_section - 2
    feeds = sec == n_section - 3
    parts = math.gcd(n_time, taps // 16)
    part_rows = taps // parts
    shares = tm < parts

    def load_w(layer):
        return pltpu.make_async_copy(
            weights.at[layer], w.at[pl.ds(layer * taps, taps)], w_sem.at[layer]
        )

    small = [
        pltpu.make_async_copy(src, dst, in_sem.at[k])
        for k, (src, dst) in enumerate(
            [
                (steps_in, timestep),
                (proj_in.at[0], proj),
                (gains_in.at[0], gains),
                (biases_in.at[0], biases),
                (clean_in, clean),
                (noise_in, noise),
                (lift_in, lift),
            ]
        )
    ]
    for copy in small[:4]:
        copy.start()

    @pl.when(first)
    def _():
        for copy in small[4:]:
            copy.start()

    barrier = pltpu.get_barrier_semaphore()

    def peers(section, begin):
        def one(r, carry):
            pl.semaphore_signal(
                barrier,
                inc=1,
                device_id=(section, lax.rem(tm + r, n_time)),
                device_id_type=MESH,
            )
            return carry

        lax.fori_loop(begin, n_time, one, 0, unroll=short)

    @pl.when(jnp.logical_not(first))
    def _():
        peers(down, 0)

    if fuse:

        @pl.when(last)
        def _():
            peers(jnp.maximum(sec - 2, 0), 0)

    peers(sec, 1)

    @pl.when(jnp.logical_not(last))
    def _():
        pl.semaphore_signal(barrier, inc=1, device_id=(up, tm), device_id_type=MESH)

    load_w(0).start()

    @pl.when(deep)
    def _():
        for layer in range(1, layers):
            load_w(layer).start()

    lanes = lax.broadcasted_iota(jnp.int32, (8, 128), 1)
    odd = lanes % 2 == 1
    upper = (lanes // 2) % 2 == 1
    far = (lanes // 4) % 2 == 1

    def swap(value, step, high):
        return jnp.where(high, pltpu.roll(value, step, 1), pltpu.roll(value, 128 - step, 1))

    def pack(s1, s2):
        wide = [
            jnp.broadcast_to(v[:, k : k + 128], (8, 128)) for v in (s1, s2) for k in (0, 128)
        ]
        one = jnp.where(odd, wide[1], wide[0]) + swap(jnp.where(odd, wide[0], wide[1]), 1, odd)
        two = jnp.where(odd, wide[3], wide[2]) + swap(jnp.where(odd, wide[2], wide[3]), 1, odd)
        both = jnp.where(upper, two, one) + swap(jnp.where(upper, one, two), 2, upper)
        return (both + swap(both, 4, far))[0:1]

    def unpack(packed):
        both = jnp.broadcast_to(packed, (8, 128))
        other = swap(both, 2, upper)
        found = []
        for pair in (jnp.where(upper, other, both), jnp.where(upper, both, other)):
            flip = swap(pair, 1, odd)
            found.append(
                jnp.concatenate([jnp.where(odd, flip, pair), jnp.where(odd, pair, flip)], axis=1)[
                    0:1
                ]
            )
        return found

    def summarize(m, kind, value, shift_row):
        shifted = value if shift_row is None else value + shift_row
        st_send[m, kind] = pack(
            jnp.sum(shifted, axis=0, keepdims=True),
            jnp.sum(shifted * shifted, axis=0, keepdims=True),
        )
        for f in range(rows_f):
            edge_send[m, kind, 0, f : f + 1, :] = value[f * frames : f * frames + 1]
            edge_send[m, kind, 1, f : f + 1, :] = value[(f + 1) * frames - 1 : (f + 1) * frames]

    def edge_copy(m, kind, lot, slot, side, section, peer):
        return pltpu.make_async_remote_copy(
            src_ref=edge_send.at[m, kind, side],
            dst_ref=edge_recv.at[m, slot, 1 - side],
            send_sem=edge_ssem.at[m, lot, side],
            recv_sem=edge_rsem.at[m, slot, 1 - side],
            device_id=(section, peer),
            device_id_type=MESH,
        )

    def publish(m, kind, lot, slot, section, begin):
        def one(r, carry):
            pltpu.make_async_remote_copy(
                src_ref=st_send.at[m, kind],
                dst_ref=st_recv.at[m, slot, tm],
                send_sem=st_ssem.at[m, lot],
                recv_sem=st_rsem.at[m, slot],
                device_id=(section, lax.rem(tm + r, n_time)),
                device_id_type=MESH,
            ).start()
            return carry

        lax.fori_loop(begin, n_time, one, 0, unroll=short)
        if begin:
            st_recv[m, slot, tm] = st_send[m, kind]

        @pl.when(has_left)
        def _():
            edge_copy(m, kind, lot, slot, 0, section, jnp.maximum(tm - 1, 0)).start()

        @pl.when(has_right)
        def _():
            edge_copy(m, kind, lot, slot, 1, section, jnp.minimum(tm + 1, n_time - 1)).start()

    def drain(m, kind, begin):
        whole = st_recv.at[m, 0, pl.ds(0, n_time - begin)]
        pltpu.make_async_copy(whole, whole, st_ssem.at[m, kind]).wait()

        @pl.when(has_left)
        def _():
            pltpu.make_async_copy(
                edge_send.at[m, 2, 0], edge_send.at[m, 2, 0], edge_ssem.at[m, kind, 0]
            ).wait()

        @pl.when(has_right)
        def _():
            pltpu.make_async_copy(
                edge_send.at[m, 2, 1], edge_send.at[m, 2, 1], edge_ssem.at[m, kind, 1]
            ).wait()

    def await_stats(m, slot, begin):
        whole = st_recv.at[m, slot, pl.ds(0, n_time - begin)]
        pltpu.make_async_copy(whole, whole, st_rsem.at[m, slot]).wait()

    def await_edges(m, slot):
        @pl.when(has_left)
        def _():
            pltpu.make_async_copy(
                edge_recv.at[m, slot, 0], edge_recv.at[m, slot, 0], edge_rsem.at[m, slot, 0]
            ).wait()

        @pl.when(has_right)
        def _():
            pltpu.make_async_copy(
                edge_recv.at[m, slot, 1], edge_recv.at[m, slot, 1], edge_rsem.at[m, slot, 1]
            ).wait()

    def convolve(m, slot, base, gain, bias, load, shift_row):
        s1, s2 = unpack(jnp.sum(st_recv[m, slot], axis=0))
        mean = s1 / count
        var = s2 / count - mean * mean
        scale = lax.rsqrt(var + 1e-05) * gain
        offset = bias - mean * scale
        edges = edge_recv[m, slot]
        if shift_row is not None:
            edges = edges + shift_row
        edges = silu(edges * scale + offset)
        before = jnp.where(has_left, edges[0], 0.0)
        after = jnp.where(has_right, edges[1], 0.0)
        place = lax.broadcasted_iota(jnp.int32, (frames, chans), 0)
        sums = [None] * rows_f

        def add(f, value):
            sums[f] = value if sums[f] is None else sums[f] + value

        hidden = load()
        act = silu(hidden * scale + offset)
        for f in range(rows_f):
            at = slice(f * frames, (f + 1) * frames)
            add(f, hidden[at])
            row = act[at]
            prev = jnp.where(place == 0, before[f : f + 1], pltpu.roll(row, 1, 0))
            nxt = jnp.where(
                place == frames - 1, after[f : f + 1], pltpu.roll(row, frames - 1, 0)
            )
            act3[at, 0:chans] = prev.astype(jnp.bfloat16)
            act3[at, chans : 2 * chans] = row.astype(jnp.bfloat16)
            act3[at, 2 * chans : 3 * chans] = nxt.astype(jnp.bfloat16)
        for i in range(3):
            used = [f for f in range(rows_f) if 0 <= f - i + 1 < rows_f]
            span = slice(used[0] * frames, (used[-1] + 1) * frames)
            tap = w[pl.ds(pl.multiple_of(base + i * 3 * chans, 16), 3 * chans), :]
            product = jnp.dot(act3[span], tap, preferred_element_type=jnp.float32)
            for k, f in enumerate(used):
                add(f - i + 1, product[k * frames : (k + 1) * frames])
        return jnp.concatenate(sums, axis=0)

    def block_copy(m, lot, section):
        return pltpu.make_async_remote_copy(
            src_ref=staged.at[m],
            dst_ref=xin.at[m],
            send_sem=blk_ssem.at[m, lot],
            recv_sem=blk_rsem.at[m],
            device_id=(section, tm),
            device_id_type=MESH,
        )

    def doubled(m):
        return fuse and m == micros - 1

    def passes(m):
        ends = jnp.logical_or(last, penult) if doubled(m) else last
        return jnp.logical_not(ends)

    def stays(m):
        return jnp.logical_or(deep, last) if doubled(m) else deep

    def finish(m, hidden):
        rounded = hidden.astype(jnp.bfloat16)
        staged[m] = rounded

        @pl.when(passes(m))
        def _():
            summarize(m, 2, rounded.astype(jnp.float32), temb_next[m : m + 1, :])
            if doubled(m):

                @pl.when(feeds)
                def _():
                    publish(m, 2, 0, 0, n_section - 1, 0)

            publish(m, 2, 2, 0, up, 0)
            if doubled(m):

                @pl.when(feeds)
                def _():
                    block_copy(m, 0, n_section - 1).start()

            block_copy(m, 1, up).start()

    def enter(m):
        @pl.when(jnp.logical_not(first))
        def _():
            await_stats(m, 0, 0)
            await_edges(m, 0)

        shift_row = temb[m : m + 1, :]
        gain, bias, base = gains[0:1, :], biases[0:1, :], 0
        if doubled(m):
            shift_row = jnp.where(last, spare[2:3, :], shift_row)
            gain = jnp.where(last, spare[0:1, :], gain)
            bias = jnp.where(last, spare[1:2, :], bias)
            base = jnp.where(last, taps, 0)

        def load():
            @pl.when(jnp.logical_not(first))
            def _():
                pltpu.make_async_copy(xin.at[m], xin.at[m], blk_rsem.at[m]).wait()

            return jnp.where(first, hmid[m], xin[m].astype(jnp.float32) + shift_row)

        hidden = convolve(m, 0, base, gain, bias, load, shift_row)

        @pl.when(stays(m))
        def _():
            kept = hidden
            if doubled(m):
                again = hidden.astype(jnp.bfloat16).astype(jnp.float32) + temb[m : m + 1, :]
                kept = jnp.where(last, again, hidden)
            hmid[m] = kept
            summarize(m, 1, kept, None)
            publish(m, 1, 1, 1, sec, 1)

        @pl.when(jnp.logical_not(stays(m)))
        def _():
            finish(m, hidden)

    def leave(m):
        @pl.when(stays(m))
        def _():
            await_stats(m, 1, 1)
            await_edges(m, 1)
            gain, bias, base = gains[1:2, :], biases[1:2, :], taps
            if doubled(m):
                gain = jnp.where(last, gains[0:1, :], gain)
                bias = jnp.where(last, biases[0:1, :], bias)
                base = jnp.where(last, 0, taps)
            finish(m, convolve(m, 1, base, gain, bias, lambda: hmid[m], None))

    for copy in small[:4]:
        copy.wait()
    half = chans // 2
    slots = temb.shape[0]
    which = lax.broadcasted_iota(jnp.int32, (slots, half), 0)
    steps_f = jnp.zeros((slots, half), jnp.float32)
    for m in range(micros):
        steps_f = jnp.where(which == m, timestep[m].astype(jnp.float32), steps_f)

    @pl.when(first)
    def _():
        level = jnp.cos(math.pi / 2.0 * (steps_f / STEPS + 0.008) / 1.008) ** 2
        keep = jnp.sqrt(level)
        blur = jnp.sqrt(1.0 - level)
        for copy in small[4:]:
            copy.wait()
        for m in range(micros):
            noisy[m * rows_f : (m + 1) * rows_f, :] = (
                keep[m : m + 1, 0:1] * clean[m] + blur[m : m + 1, 0:1] * noise[m]
            )

    order = lax.broadcasted_iota(jnp.int32, (slots, half), 1).astype(jnp.float32)
    angles = steps_f * jnp.exp(-math.log(10000.0) * order / half)
    temb[...] = jnp.dot(
        jnp.sin(angles).astype(jnp.bfloat16), proj[0:half, :], preferred_element_type=jnp.float32
    ) + jnp.dot(
        jnp.cos(angles).astype(jnp.bfloat16), proj[half:chans, :], preferred_element_type=jnp.float32
    )

    arrivals = n_time - 1 + n_time * jnp.where(last, 0, 1) + jnp.where(first, 0, 1)
    if fuse:
        arrivals = arrivals + n_time * jnp.where(feeds, 1, 0)
    pl.semaphore_wait(barrier, arrivals)

    def tell(r, carry):
        pltpu.make_async_remote_copy(
            src_ref=noisy,
            dst_ref=heard.at[tm],
            send_sem=heard_ssem,
            recv_sem=heard_rsem,
            device_id=(sec, lax.rem(tm + r, n_time)),
            device_id_type=MESH,
        ).start()
        return carry

    @pl.when(first)
    def _():
        lax.fori_loop(1, n_time, tell, 0, unroll=short)

    pass_temb = pltpu.make_async_remote_copy(
        src_ref=temb,
        dst_ref=temb_next,
        send_sem=temb_ssem,
        recv_sem=temb_rsem,
        device_id=(down, tm),
        device_id_type=MESH,
    )

    @pl.when(jnp.logical_not(first))
    def _():
        pass_temb.start()

    load_w(0).wait()

    @pl.when(deep)
    def _():
        for layer in range(1, layers):
            load_w(layer).wait()

    mine = pl.ds(pl.multiple_of(taps + tm * part_rows, 16), part_rows)
    pass_part = pltpu.make_async_remote_copy(
        src_ref=w.at[pl.ds(pl.multiple_of(tm * part_rows, 16), part_rows)],
        dst_ref=w.at[mine],
        send_sem=part_ssem,
        recv_sem=part_rsem,
        device_id=(up, tm),
        device_id_type=MESH,
    )
    pass_spare = pltpu.make_async_remote_copy(
        src_ref=spare_send,
        dst_ref=spare,
        send_sem=spare_ssem,
        recv_sem=spare_rsem,
        device_id=(up, tm),
        device_id_type=MESH,
    )

    def share(r, carry):
        pltpu.make_async_remote_copy(
            src_ref=w.at[mine],
            dst_ref=w.at[mine],
            send_sem=share_ssem,
            recv_sem=share_rsem,
            device_id=(sec, lax.rem(tm + r, n_time)),
            device_id_type=MESH,
        ).start()
        return carry

    def await_rows(count_rows, sem):
        whole = w.at[pl.ds(0, count_rows)]
        pltpu.make_async_copy(whole, whole, sem).wait()

    if fuse:

        @pl.when(penult)
        def _():
            spare_send[...] = jnp.zeros_like(spare_send)
            spare_send[0:1, :] = gains[0:1, :]
            spare_send[1:2, :] = biases[0:1, :]
            spare_send[2:3, :] = temb[micros - 1 : micros, :]
            pass_spare.start()

            @pl.when(shares)
            def _():
                pass_part.start()

        @pl.when(last)
        def _():
            @pl.when(shares)
            def _():
                pass_part.wait_recv()
                lax.fori_loop(1, n_time, share, 0, unroll=short)
                await_rows((parts - 1) * part_rows, share_rsem)

            @pl.when(jnp.logical_not(shares))
            def _():
                await_rows(parts * part_rows, share_rsem)

            pltpu.make_async_copy(spare, spare, spare_rsem).wait()

    @pl.when(first)
    def _():
        columns = jnp.transpose(noisy[...])
        for m in range(micros):
            for f in range(rows_f):
                at = m * rows_f + f
                hmid[m, f * frames : (f + 1) * frames, :] = (
                    columns[:, at : at + 1] * lift[...] + temb[m : m + 1, :]
                )
        others = heard.at[pl.ds(0, n_time - 1)]
        pltpu.make_async_copy(others, others, heard_rsem).wait()
        heard[tm] = noisy[...]
        everywhere = heard[...]
        flat1 = jnp.sum(jnp.sum(everywhere, axis=0), axis=1, keepdims=True)
        flat2 = jnp.sum(jnp.sum(everywhere * everywhere, axis=0), axis=1, keepdims=True)
        beyond = (
            heard[jnp.maximum(tm - 1, 0)][:, frames - 1 : frames],
            heard[jnp.minimum(tm + 1, n_time - 1)][:, 0:1],
        )
        for m in range(micros):
            at = slice(m * rows_f, (m + 1) * rows_f)
            total1 = jnp.sum(flat1[at], axis=0, keepdims=True)
            total2 = jnp.sum(flat2[at], axis=0, keepdims=True)
            shift_row = temb[m : m + 1, :]
            gained = lift[...] * total1
            st_recv[m, 0] = jnp.zeros_like(st_recv[m, 0])
            st_recv[m, 0, 0] = pack(
                gained + positions * shift_row,
                lift[...] * (lift[...] * total2)
                + 2.0 * shift_row * gained
                + positions * (shift_row * shift_row),
            )
            for side in range(2):
                edge_recv[m, 0, side] = beyond[side][at] * lift[...]

    @pl.when(jnp.logical_not(last))
    def _():
        pltpu.make_async_copy(temb_next, temb_next, temb_rsem).wait()

    enter(0)
    for m in range(1, micros):
        enter(m)
        leave(m - 1)
    leave(micros - 1)

    @pl.when(first)
    def _():
        others = heard.at[pl.ds(0, n_time - 1)]
        pltpu.make_async_copy(others, others, heard_ssem).wait()

    @pl.when(jnp.logical_not(first))
    def _():
        pass_temb.wait_send()

    if fuse:

        @pl.when(penult)
        def _():
            pass_spare.wait_send()

            @pl.when(shares)
            def _():
                pass_part.wait_send()

        @pl.when(jnp.logical_and(last, shares))
        def _():
            await_rows((n_time - 1) * part_rows, share_ssem)

    for m in range(micros):

        @pl.when(stays(m))
        def _():
            drain(m, 1, 1)

        if doubled(m):

            @pl.when(feeds)
            def _():
                drain(m, 0, 0)
                block_copy(m, 0, n_section - 1).wait_send()

        @pl.when(passes(m))
        def _():
            drain(m, 2, 0)
            block_copy(m, 1, up).wait_send()


def on_device(clean, noise, timestep, lift, norm_gain, norm_bias, conv_weight, time_proj):
    n_time = lax.axis_size("tm")
    n_section = lax.axis_size("section")
    micros, rows_f, frames = clean.shape
    chans = lift.shape[0]
    layers = norm_gain.shape[1]
    slots = -(-micros // 8) * 8
    rows = rows_f * frames
    fuse = n_section - 2 >= max(n_section // 2, 1) and layers > 1
    dims = (n_time, n_section, micros, rows_f, frames, chans, layers, fuse)
    vmem = pl.BlockSpec(memory_space=pltpu.VMEM)
    hbm = pl.BlockSpec(memory_space=pl.ANY)
    dma = pltpu.SemaphoreType.DMA
    saved = pl.pallas_call(
        functools.partial(kernel, dims),
        out_shape=pltpu.VMEM((micros, rows, chans), jnp.bfloat16),
        in_specs=[hbm] * 8,
        out_specs=vmem,
        scratch_shapes=[
            pltpu.VMEM((layers * 9 * chans, chans), jnp.bfloat16),
            pltpu.VMEM((micros, rows, chans), jnp.bfloat16),
            pltpu.VMEM((micros, rows, chans), jnp.float32),
            pltpu.VMEM((n_time, micros * rows_f, frames), jnp.float32),
            pltpu.VMEM((slots, chans), jnp.float32),
            pltpu.VMEM((8, chans), jnp.float32),
            pltpu.VMEM((8, chans), jnp.float32),
            pltpu.VMEM((micros, rows_f, frames), jnp.float32),
            pltpu.VMEM((micros, rows_f, frames), jnp.float32),
            pltpu.VMEM((1, chans), jnp.float32),
            pltpu.VMEM((layers, chans), jnp.float32),
            pltpu.VMEM((layers, chans), jnp.float32),
            pltpu.VMEM((chans, chans), jnp.bfloat16),
            pltpu.VMEM((micros * rows_f, frames), jnp.float32),
            pltpu.VMEM((slots, chans), jnp.float32),
            pltpu.SMEM((micros,), jnp.int32),
            pltpu.VMEM((rows, 3 * chans), jnp.bfloat16),
            pltpu.VMEM((micros, 3, 1, 128), jnp.float32),
            pltpu.VMEM((micros, 2, n_time, 1, 128), jnp.float32),
            pltpu.VMEM((micros, 3, 2, rows_f, chans), jnp.float32),
            pltpu.VMEM((micros, 2, 2, rows_f, chans), jnp.float32),
            dma((micros, 3)),
            dma((micros, 2)),
            dma((micros, 3, 2)),
            dma((micros, 2, 2)),
            dma((micros, 2)),
            dma((micros,)),
            dma((layers,)),
            dma((7,)),
            *[dma] * 10,
        ],
        compiler_params=pltpu.CompilerParams(
            collective_id=0, has_side_effects=True, vmem_limit_bytes=48 * 2**20
        ),
    )(
        *(
            pltpu.with_memory_space_constraint(x, pltpu.HBM)
            for x in (
                timestep,
                clean,
                noise,
                lift.reshape(1, chans),
                norm_gain,
                norm_bias,
                time_proj,
                conv_weight.reshape(layers, 9 * chans, chans),
            )
        ),
    )
    return saved.reshape(1, micros, rows_f, frames, chans)


def solution(mesh):
    in_specs = (
        P(None, None, "tm"),
        P(None, None, "tm"),
        P(),
        P(),
        P("section", None, None),
        P("section", None, None),
        P("section", None, None, None, None, None),
        P("section", None, None),
    )
    out_specs = P("section", None, None, "tm", None)
    return jax.shard_map(
        on_device, mesh=mesh, in_specs=in_specs, out_specs=out_specs, check_vma=False
    )
```

```python
import functools
import math

import jax
import jax.numpy as jnp
from jax import lax
from jax.experimental import pallas as pl
from jax.experimental.pallas import tpu as pltpu
from jax.sharding import PartitionSpec as P

GROUPS = 32
STEPS = 1000
LEAD = 1
MESH = pl.DeviceIdType.MESH


def silu(z):
    half = 0.5 * z
    return half + half * jnp.tanh(half)


def kernel(
    dims,
    steps_in,
    clean_in,
    noise_in,
    lift_in,
    gains_in,
    biases_in,
    proj_in,
    weights,
    staged,
    w,
    xin,
    hmid,
    noisy,
    told,
    heard,
    temb_next,
    clean,
    noise,
    lift,
    gains,
    biases,
    proj,
    temb,
    timestep,
    act3,
    letter,
    box,
    tally,
    let_ssem,
    let_rsem,
    blk_ssem,
    blk_rsem,
    w_sem,
    in_sem,
    heard_ssem,
    heard_rsem,
    temb_ssem,
    temb_rsem,
    ready,
):
    n_time, n_section, micros, rows_f, frames, chans, layers = dims
    rows = rows_f * frames
    positions = rows * n_time
    width = chans // GROUPS
    count = positions * width
    halves = chans // 128
    edge_rows = rows_f * halves
    sec = lax.axis_index("section")
    tm = lax.axis_index("tm")
    deep = sec < n_section // 2
    first = sec == 0
    last = sec == n_section - 1
    has_left = tm > 0
    has_right = tm < n_time - 1
    left = jnp.maximum(tm - 1, 0)
    right = jnp.minimum(tm + 1, n_time - 1)
    up = jnp.minimum(sec + 1, n_section - 1)
    down = jnp.maximum(sec - 1, 0)
    short = n_time <= 8

    def each(begin, end, one):
        def step(r, carry):
            one(lax.rem(tm + r, n_time))
            return carry

        lax.fori_loop(begin, end, step, 0, unroll=short)

    def load_w(layer):
        return pltpu.make_async_copy(weights.at[layer], w.at[layer], w_sem.at[layer])

    small = [
        pltpu.make_async_copy(src, dst, in_sem.at[k])
        for k, (src, dst) in enumerate(
            [
                (steps_in, timestep),
                (proj_in.at[0], proj),
                (gains_in.at[0], gains),
                (biases_in.at[0], biases),
                (clean_in, clean),
                (noise_in, noise),
                (lift_in, lift),
            ]
        )
    ]

    barrier = pltpu.get_barrier_semaphore()

    def greet(section):
        def one(peer):
            pl.semaphore_signal(
                barrier, inc=1, device_id=(section, peer), device_id_type=MESH
            )

        return one

    each(1, n_time, greet(sec))

    for copy in small[:4]:
        copy.start()

    @pl.when(first)
    def _():
        for copy in small[4:]:
            copy.start()

    @pl.when(jnp.logical_not(last))
    def _():
        each(0, n_time, greet(up))

    load_w(0).start()

    @pl.when(deep)
    def _():
        for layer in range(1, layers):
            load_w(layer).start()

    lanes = lax.broadcasted_iota(jnp.int32, (8, 128), 1)
    tiers = lax.broadcasted_iota(jnp.int32, (8, 128), 0)
    spot = lanes % width
    quad = lanes % 4

    def turn(value, step):
        return value if step == 0 else pltpu.roll(value, step % 128, 1)

    def pack(s1, s2):
        tall = jnp.where(
            tiers < 2,
            jnp.where(tiers == 0, s1[:, 0:128], s1[:, 128:256]),
            jnp.where(tiers == 2, s2[:, 0:128], s2[:, 128:256]),
        )
        total = tall
        for r in range(1, width):
            total = total + jnp.where(spot < width - r, turn(tall, -r), turn(tall, width - r))
        return jnp.sum(jnp.where(tiers == quad, total, 0.0), axis=0, keepdims=True)

    def unpack(packed):
        wide = jnp.broadcast_to(packed, (8, 128))
        turned = {k: turn(wide, k) for k in range(-3, 4)}
        found = []
        for v in range(4):
            low = jnp.where(quad == 0, turned[-v], turned[1 - v])
            high = jnp.where(quad == 2, turned[2 - v], turned[3 - v])
            found.append(jnp.where(quad < 2, low, high)[0:1])
        return found

    def summarize(m, kind, value):
        stats = pack(
            jnp.sum(value, axis=0, keepdims=True), jnp.sum(value * value, axis=0, keepdims=True)
        )
        for side in range(2):
            for f in range(rows_f):
                at = f * frames + side * (frames - 1)
                for k in range(halves):
                    letter[m, kind, side, k * rows_f + f] = value[
                        at : at + 1, k * 128 : (k + 1) * 128
                    ]
            letter[m, kind, side, edge_rows] = stats

    def post(m, kind, side, begin, rows_sent, section, peer):
        pltpu.make_async_remote_copy(
            src_ref=letter.at[m, kind, side, pl.ds(begin, rows_sent)],
            dst_ref=box.at[m, 1 - kind, tm, pl.ds(begin, rows_sent)],
            send_sem=let_ssem.at[m, kind],
            recv_sem=let_rsem.at[m, 1 - kind],
            device_id=(section, peer),
            device_id_type=MESH,
        ).start()

    def publish(m, kind, section, begin):
        def plain(peer):
            post(m, kind, 0, edge_rows, 1, section, peer)

        each(2, n_time - 1, plain)

        @pl.when(has_right)
        def _():
            post(m, kind, 1, 0, edge_rows + 1, section, right)

        @pl.when(has_left)
        def _():
            post(m, kind, 0, 0, edge_rows + 1, section, left)

        if n_time > 2:

            @pl.when(jnp.logical_not(has_right))
            def _():
                plain(0)

            @pl.when(jnp.logical_not(has_left))
            def _():
                plain(n_time - 1)

        if begin == 0:
            plain(tm)
        else:
            box[m, 1 - kind, tm, edge_rows] = letter[m, kind, 0, edge_rows]

    def await_letters(sem, begin):
        plain = n_time - begin

        def take(long):
            whole = tally.at[pl.ds(0, plain + long * edge_rows)]
            pltpu.make_async_copy(whole, whole, sem).wait()

        if n_time > 2:
            both = jnp.logical_and(has_left, has_right)

            @pl.when(both)
            def _():
                take(2)

            @pl.when(jnp.logical_not(both))
            def _():
                take(1)

        elif n_time == 2:
            take(1)
        elif plain:
            take(0)

    def convolve(m, slot, layer, load):
        posts = box[m, slot, :, edge_rows]
        low1, high1, low2, high2 = unpack(jnp.sum(posts, axis=0))
        scales, offsets = [], []
        for k, (s1, s2) in enumerate([(low1, low2), (high1, high2)]):
            at = slice(k * 128, (k + 1) * 128)
            mean = s1 / count
            var = s2 / count - mean * mean
            scale = lax.rsqrt(var + 1e-05) * gains[layer : layer + 1, at]
            scales.append(scale)
            offsets.append(biases[layer : layer + 1, at] - mean * scale)
        scale = jnp.concatenate(scales, axis=1)
        offset = jnp.concatenate(offsets, axis=1)
        beyond = []
        for near, there in ((left, has_left), (right, has_right)):
            tall = jnp.concatenate([box[m, slot, near, r] for r in range(edge_rows)], axis=0)
            parts = [
                silu(tall[k * rows_f : (k + 1) * rows_f] * scales[k] + offsets[k])
                for k in range(halves)
            ]
            beyond.append(jnp.where(there, jnp.concatenate(parts, axis=1), 0.0))
        before, after = beyond
        place = lax.broadcasted_iota(jnp.int32, (frames, chans), 0)
        sums = [None] * rows_f

        def add(f, value):
            sums[f] = value if sums[f] is None else sums[f] + value

        hidden = load()
        act = silu(hidden * scale + offset)
        for f in range(rows_f):
            at = slice(f * frames, (f + 1) * frames)
            add(f, hidden[at])
            row = act[at]
            prev = jnp.where(place == 0, before[f : f + 1], pltpu.roll(row, 1, 0))
            nxt = jnp.where(
                place == frames - 1, after[f : f + 1], pltpu.roll(row, frames - 1, 0)
            )
            act3[at, 0:chans] = prev.astype(jnp.bfloat16)
            act3[at, chans : 2 * chans] = row.astype(jnp.bfloat16)
            act3[at, 2 * chans : 3 * chans] = nxt.astype(jnp.bfloat16)
        for i in range(3):
            used = [f for f in range(rows_f) if 0 <= f - i + 1 < rows_f]
            span = slice(used[0] * frames, (used[-1] + 1) * frames)
            product = jnp.dot(act3[span], w[layer, i], preferred_element_type=jnp.float32)
            for k, f in enumerate(used):
                add(f - i + 1, product[k * frames : (k + 1) * frames])
        return jnp.concatenate(sums, axis=0)

    def block_copy(m, begin, end):
        span = pl.ds(begin * frames, (end - begin) * frames)
        return pltpu.make_async_remote_copy(
            src_ref=staged.at[m, span],
            dst_ref=xin.at[m, span],
            send_sem=blk_ssem.at[m],
            recv_sem=blk_rsem.at[m],
            device_id=(up, tm),
            device_id_type=MESH,
        )

    def finish(m, hidden):
        rounded = hidden.astype(jnp.bfloat16)
        staged[m] = rounded

        @pl.when(jnp.logical_not(last))
        def _():
            block_copy(m, 0, LEAD).start()
            summarize(m, 1, rounded.astype(jnp.float32) + temb_next[m : m + 1, :])
            publish(m, 1, up, 0)
            block_copy(m, LEAD, rows_f).start()

    def enter(m):
        @pl.when(jnp.logical_not(first))
        def _():
            await_letters(let_rsem.at[m, 0], 0)

        def load():
            @pl.when(jnp.logical_not(first))
            def _():
                pltpu.make_async_copy(xin.at[m], xin.at[m], blk_rsem.at[m]).wait()

            return jnp.where(
                first, hmid[m], xin[m].astype(jnp.float32) + temb[m : m + 1, :]
            )

        hidden = convolve(m, 0, 0, load)

        @pl.when(deep)
        def _():
            hmid[m] = hidden
            summarize(m, 0, hidden)
            publish(m, 0, sec, 1)

        @pl.when(jnp.logical_not(deep))
        def _():
            finish(m, hidden)

    def leave(m):
        @pl.when(deep)
        def _():
            await_letters(let_rsem.at[m, 1], 1)
            finish(m, convolve(m, 1, 1, lambda: hmid[m]))

    for copy in small[:4]:
        copy.wait()
    half = chans // 2
    slots = temb.shape[0]
    which = lax.broadcasted_iota(jnp.int32, (slots, half), 0)
    steps_f = jnp.zeros((slots, half), jnp.float32)
    for m in range(micros):
        steps_f = jnp.where(which == m, timestep[m].astype(jnp.float32), steps_f)

    @pl.when(first)
    def _():
        level = jnp.cos(math.pi / 2.0 * (steps_f / STEPS + 0.008) / 1.008) ** 2
        keep = jnp.sqrt(level)
        blur = jnp.sqrt(1.0 - level)
        for copy in small[4:]:
            copy.wait()
        column = lax.broadcasted_iota(jnp.int32, (rows_f, 128), 1)
        for m in range(micros):
            mixed = keep[m : m + 1, 0:1] * clean[m] + blur[m : m + 1, 0:1] * noise[m]
            at = slice(m * rows_f, (m + 1) * rows_f)
            noisy[at, :] = mixed
            flat1 = jnp.sum(mixed, axis=1, keepdims=True)
            flat2 = jnp.sum(mixed * mixed, axis=1, keepdims=True)
            told[at, :] = jnp.where(
                column < 2,
                jnp.where(column == 0, flat1, flat2),
                jnp.where(column == 2, mixed[:, 0:1], mixed[:, frames - 1 : frames]),
            )

    order = lax.broadcasted_iota(jnp.int32, (slots, half), 1).astype(jnp.float32)
    angles = steps_f * jnp.exp(-math.log(10000.0) * order / half)
    temb[...] = jnp.dot(
        jnp.sin(angles).astype(jnp.bfloat16), proj[0:half, :], preferred_element_type=jnp.float32
    ) + jnp.dot(
        jnp.cos(angles).astype(jnp.bfloat16), proj[half:chans, :], preferred_element_type=jnp.float32
    )

    pl.semaphore_wait(barrier, n_time - 1 + n_time * jnp.where(first, 0, 1))

    def tell(peer):
        pltpu.make_async_remote_copy(
            src_ref=told,
            dst_ref=heard.at[tm],
            send_sem=heard_ssem,
            recv_sem=heard_rsem,
            device_id=(sec, peer),
            device_id_type=MESH,
        ).start()

    def invite(peer):
        pl.semaphore_signal(ready, inc=1, device_id=(down, peer), device_id_type=MESH)

    pass_temb = pltpu.make_async_remote_copy(
        src_ref=temb,
        dst_ref=temb_next,
        send_sem=temb_ssem,
        recv_sem=temb_rsem,
        device_id=(down, tm),
        device_id_type=MESH,
    )

    @pl.when(first)
    def _():
        each(1, n_time, tell)

    @pl.when(jnp.logical_not(first))
    def _():
        each(0, n_time, invite)
        pass_temb.start()

    load_w(0).wait()

    @pl.when(deep)
    def _():
        for layer in range(1, layers):
            load_w(layer).wait()

    @pl.when(first)
    def _():
        columns = jnp.transpose(noisy[...])
        for m in range(micros):
            for f in range(rows_f):
                at = m * rows_f + f
                hmid[m, f * frames : (f + 1) * frames, :] = (
                    columns[:, at : at + 1] * lift[...] + temb[m : m + 1, :]
                )
        heard[tm] = told[...]
        fixed = []
        for m in range(micros):
            shift = temb[m : m + 1, :]
            fixed.append(
                (
                    pack(lift[...], 2.0 * lift[...] * shift),
                    pack(jnp.zeros_like(shift), lift[...] * lift[...]),
                    pack(positions * shift, positions * (shift * shift)),
                )
            )
            box[m, 0, :, edge_rows] = jnp.zeros_like(box[m, 0, :, edge_rows])
        if n_time > 1:
            others = heard.at[pl.ds(0, n_time - 1)]
            pltpu.make_async_copy(others, others, heard_rsem).wait()
        total = jnp.sum(heard[...], axis=0)
        near = (heard[left][:, 3:4], heard[right][:, 2:3])
        for m in range(micros):
            at = slice(m * rows_f, (m + 1) * rows_f)
            flat = jnp.sum(total[at], axis=0, keepdims=True)
            by1, by2, alone = fixed[m]
            box[m, 0, 0, edge_rows] = by1 * flat[:, 0:1] + by2 * flat[:, 1:2] + alone
            for side, peer in ((0, left), (1, right)):
                edge = near[side][at] * lift[...] + temb[m : m + 1, :]
                for f in range(rows_f):
                    for k in range(halves):
                        box[m, 0, peer, k * rows_f + f] = edge[
                            f : f + 1, k * 128 : (k + 1) * 128
                        ]

    @pl.when(jnp.logical_not(last))
    def _():
        pltpu.make_async_copy(temb_next, temb_next, temb_rsem).wait()
        pl.semaphore_wait(ready, n_time)

    enter(0)
    for m in range(1, micros):
        enter(m)
        leave(m - 1)
    leave(micros - 1)

    @pl.when(first)
    def _():
        if n_time > 1:
            others = heard.at[pl.ds(0, n_time - 1)]
            pltpu.make_async_copy(others, others, heard_ssem).wait()

    @pl.when(jnp.logical_not(first))
    def _():
        pass_temb.wait_send()

    @pl.when(deep)
    def _():
        for m in range(micros):
            await_letters(let_ssem.at[m, 0], 1)

    @pl.when(jnp.logical_not(last))
    def _():
        for m in range(micros):
            await_letters(let_ssem.at[m, 1], 0)
            pltpu.make_async_copy(staged.at[m], staged.at[m], blk_ssem.at[m]).wait()


def on_device(clean, noise, timestep, lift, norm_gain, norm_bias, conv_weight, time_proj):
    n_time = lax.axis_size("tm")
    n_section = lax.axis_size("section")
    micros, rows_f, frames = clean.shape
    chans = lift.shape[0]
    layers = norm_gain.shape[1]
    slots = -(-micros // 8) * 8
    rows = rows_f * frames
    dims = (n_time, n_section, micros, rows_f, frames, chans, layers)
    letter_rows = rows_f * (chans // 128) + 1
    vmem = pl.BlockSpec(memory_space=pltpu.VMEM)
    hbm = pl.BlockSpec(memory_space=pl.ANY)
    dma = pltpu.SemaphoreType.DMA
    saved = pl.pallas_call(
        functools.partial(kernel, dims),
        out_shape=pltpu.VMEM((micros, rows, chans), jnp.bfloat16),
        in_specs=[hbm] * 8,
        out_specs=vmem,
        scratch_shapes=[
            pltpu.VMEM((layers, 3, 3 * chans, chans), jnp.bfloat16),
            pltpu.VMEM((micros, rows, chans), jnp.bfloat16),
            pltpu.VMEM((micros, rows, chans), jnp.float32),
            pltpu.VMEM((micros * rows_f, frames), jnp.float32),
            pltpu.VMEM((micros * rows_f, 128), jnp.float32),
            pltpu.VMEM((n_time, micros * rows_f, 128), jnp.float32),
            pltpu.VMEM((slots, chans), jnp.float32),
            pltpu.VMEM((micros, rows_f, frames), jnp.float32),
            pltpu.VMEM((micros, rows_f, frames), jnp.float32),
            pltpu.VMEM((1, chans), jnp.float32),
            pltpu.VMEM((layers, chans), jnp.float32),
            pltpu.VMEM((layers, chans), jnp.float32),
            pltpu.VMEM((chans, chans), jnp.bfloat16),
            pltpu.VMEM((slots, chans), jnp.float32),
            pltpu.SMEM((micros,), jnp.int32),
            pltpu.VMEM((rows, 3 * chans), jnp.bfloat16),
            pltpu.VMEM((micros, 2, 2, letter_rows, 1, 128), jnp.float32),
            pltpu.VMEM((micros, 2, n_time, letter_rows, 1, 128), jnp.float32),
            pltpu.VMEM((n_time + 2 * letter_rows, 1, 128), jnp.float32),
            dma((micros, 2)),
            dma((micros, 2)),
            dma((micros,)),
            dma((micros,)),
            dma((layers,)),
            dma((7,)),
            dma,
            dma,
            dma,
            dma,
            pltpu.SemaphoreType.REGULAR,
        ],
        compiler_params=pltpu.CompilerParams(
            collective_id=0, has_side_effects=True, vmem_limit_bytes=48 * 2**20
        ),
    )(
        *(
            pltpu.with_memory_space_constraint(x, pltpu.HBM)
            for x in (
                timestep,
                clean,
                noise,
                lift.reshape(1, chans),
                norm_gain,
                norm_bias,
                time_proj,
                conv_weight.reshape(layers, 3, 3 * chans, chans),
            )
        ),
    )
    return saved.reshape(1, micros, rows_f, frames, chans)


def solution(mesh):
    in_specs = (
        P(None, None, "tm"),
        P(None, None, "tm"),
        P(),
        P(),
        P("section", None, None),
        P("section", None, None),
        P("section", None, None, None, None, None),
        P("section", None, None),
    )
    out_specs = P("section", None, None, "tm", None)
    return jax.shard_map(
        on_device, mesh=mesh, in_specs=in_specs, out_specs=out_specs, check_vma=False
    )
```

```python
import functools
import math

import jax
import jax.numpy as jnp
from jax import lax
from jax.experimental import pallas as pl
from jax.experimental.pallas import tpu as pltpu
from jax.sharding import PartitionSpec as P

GROUPS = 32
STEPS = 1000
LEAD = 1
FIRST = 3
MESH = pl.DeviceIdType.MESH


def silu(half):
    return half + half * jnp.tanh(half)


def kernel(
    dims,
    steps_in,
    clean_in,
    noise_in,
    lift_in,
    gains_in,
    biases_in,
    proj_in,
    weights,
    staged,
    w,
    xin,
    hmid,
    noisy,
    told,
    heard,
    temb_next,
    clean,
    noise,
    lift,
    gains,
    biases,
    proj,
    temb,
    timestep,
    act3,
    letter,
    box,
    tally,
    let_ssem,
    let_rsem,
    blk_ssem,
    blk_rsem,
    w_sem,
    in_sem,
    heard_ssem,
    heard_rsem,
    temb_ssem,
    temb_rsem,
    ready,
):
    n_time, n_section, micros, rows_f, frames, chans, layers = dims
    rows = rows_f * frames
    positions = rows * n_time
    width = chans // GROUPS
    count = positions * width
    halves = chans // 128
    edge_rows = rows_f * halves
    sec = lax.axis_index("section")
    tm = lax.axis_index("tm")
    deep = sec < n_section // 2
    first = sec == 0
    last = sec == n_section - 1
    has_left = tm > 0
    has_right = tm < n_time - 1
    left = jnp.maximum(tm - 1, 0)
    right = jnp.minimum(tm + 1, n_time - 1)
    up = jnp.minimum(sec + 1, n_section - 1)
    down = jnp.maximum(sec - 1, 0)
    short = n_time <= 8

    def each(begin, end, one):
        def step(r, carry):
            one(lax.rem(tm + r, n_time))
            return carry

        lax.fori_loop(begin, end, step, 0, unroll=short)

    def load_w(layer):
        return pltpu.make_async_copy(weights.at[layer], w.at[layer], w_sem.at[layer])

    small = [
        pltpu.make_async_copy(src, dst, in_sem.at[k])
        for k, (src, dst) in enumerate(
            [
                (steps_in, timestep),
                (proj_in.at[0], proj),
                (gains_in.at[0], gains),
                (biases_in.at[0], biases),
                (clean_in, clean),
                (noise_in, noise),
                (lift_in, lift),
            ]
        )
    ]

    barrier = pltpu.get_barrier_semaphore()

    def greet(section):
        def one(peer):
            pl.semaphore_signal(
                barrier, inc=1, device_id=(section, peer), device_id_type=MESH
            )

        return one

    each(1, n_time, greet(sec))

    for copy in small[:4]:
        copy.start()

    @pl.when(first)
    def _():
        for copy in small[4:]:
            copy.start()

    @pl.when(jnp.logical_not(last))
    def _():
        each(0, n_time, greet(up))

    load_w(0).start()

    @pl.when(deep)
    def _():
        for layer in range(1, layers):
            load_w(layer).start()

    lanes = lax.broadcasted_iota(jnp.int32, (8, 128), 1)
    tiers = lax.broadcasted_iota(jnp.int32, (8, 128), 0)
    spot = lanes % width
    quad = lanes % 4

    def turn(value, step):
        return value if step == 0 else pltpu.roll(value, step % 128, 1)

    def group_total(tall):
        total = tall
        for r in range(1, width):
            total = total + jnp.where(spot < width - r, turn(tall, -r), turn(tall, width - r))
        return total

    def pack(s1, s2):
        tall = jnp.where(
            tiers < 2,
            jnp.where(tiers == 0, s1[:, 0:128], s1[:, 128:256]),
            jnp.where(tiers == 2, s2[:, 0:128], s2[:, 128:256]),
        )
        total = group_total(tall)
        return jnp.sum(jnp.where(tiers == quad, total, 0.0), axis=0, keepdims=True)

    def spread(stats):
        tall = jnp.where(
            tiers < 2,
            jnp.where(tiers == 0, stats[0], stats[1]),
            jnp.where(tiers == 2, stats[2], stats[3]),
        )
        total = group_total(tall)
        return [total[k : k + 1] for k in range(2 * halves)]

    def unpack(packed):
        wide = jnp.broadcast_to(packed, (8, 128))
        turned = {k: turn(wide, k) for k in range(-3, 4)}
        found = []
        for v in range(4):
            low = jnp.where(quad == 0, turned[-v], turned[1 - v])
            high = jnp.where(quad == 2, turned[2 - v], turned[3 - v])
            found.append(jnp.where(quad < 2, low, high)[0:1])
        return found

    def summarize(m, kind, value):
        s1 = jnp.sum(value, axis=0, keepdims=True)
        s2 = jnp.sum(value * value, axis=0, keepdims=True)
        if kind:
            stats = [pack(s1, s2)]
        else:
            stats = [v[:, k * 128 : (k + 1) * 128] for v in (s1, s2) for k in range(halves)]
        for side in range(2):
            for f in range(rows_f):
                at = f * frames + side * (frames - 1)
                for k in range(halves):
                    letter[m, kind, side, k * rows_f + f] = value[
                        at : at + 1, k * 128 : (k + 1) * 128
                    ]
            for k, stat in enumerate(stats):
                letter[m, kind, side, edge_rows + k] = stat

    def post(m, kind, side, begin, rows_sent, section, peer):
        pltpu.make_async_remote_copy(
            src_ref=letter.at[m, kind, side, pl.ds(begin, rows_sent)],
            dst_ref=box.at[m, 1 - kind, tm, pl.ds(begin, rows_sent)],
            send_sem=let_ssem.at[m, kind],
            recv_sem=let_rsem.at[m, 1 - kind],
            device_id=(section, peer),
            device_id_type=MESH,
        ).start()

    stat_rows = (2 * halves, 1)

    def publish(m, kind, section):
        span = stat_rows[kind]

        def plain(peer):
            post(m, kind, 0, edge_rows, span, section, peer)

        each(2, n_time - 1, plain)

        @pl.when(has_right)
        def _():
            post(m, kind, 1, 0, edge_rows + span, section, right)

        @pl.when(has_left)
        def _():
            post(m, kind, 0, 0, edge_rows + span, section, left)

        if n_time > 2:

            @pl.when(jnp.logical_not(has_right))
            def _():
                plain(0)

            @pl.when(jnp.logical_not(has_left))
            def _():
                plain(n_time - 1)

        if kind:
            plain(tm)
        else:
            for k in range(span):
                box[m, 1, tm, edge_rows + k] = letter[m, 0, 0, edge_rows + k]

    def await_letters(sem, kind):
        plain = (n_time if kind else n_time - 1) * stat_rows[kind]

        def take(long):
            whole = tally.at[pl.ds(0, plain + long * edge_rows)]
            pltpu.make_async_copy(whole, whole, sem).wait()

        if n_time > 2:
            both = jnp.logical_and(has_left, has_right)

            @pl.when(both)
            def _():
                take(2)

            @pl.when(jnp.logical_not(both))
            def _():
                take(1)

        elif n_time == 2:
            take(1)
        elif plain:
            take(0)

    def convolve(m, layer, stats, stages, load):
        low1, high1, low2, high2 = stats
        gain = gains[pl.ds(layer, 1), :]
        bias = biases[pl.ds(layer, 1), :]
        scales, offsets = [], []
        for k, (s1, s2) in enumerate([(low1, low2), (high1, high2)]):
            at = slice(k * 128, (k + 1) * 128)
            mean = s1 / count
            var = s2 / count - mean * mean
            scale = lax.rsqrt(var + 1e-05) * (0.5 * gain[:, at])
            scales.append(scale)
            offsets.append(0.5 * bias[:, at] - mean * scale)
        scale = jnp.concatenate(scales, axis=1)
        offset = jnp.concatenate(offsets, axis=1)
        beyond = []
        for near, there in ((left, has_left), (right, has_right)):
            tall = jnp.concatenate([box[m, layer, near, r] for r in range(edge_rows)], axis=0)
            parts = [
                silu(tall[k * rows_f : (k + 1) * rows_f] * scales[k] + offsets[k])
                for k in range(halves)
            ]
            beyond.append(jnp.where(there, jnp.concatenate(parts, axis=1), 0.0))
        before, after = beyond
        place = lax.broadcasted_iota(jnp.int32, (frames, chans), 0)
        sums = [None] * rows_f

        def add(f, value):
            sums[f] = value if sums[f] is None else sums[f] + value

        for low, high, taps in stages:
            hidden = load(low, high)
            act = silu(hidden * scale + offset)
            for f in range(low, high):
                at = slice((f - low) * frames, (f - low + 1) * frames)
                add(f, hidden[at])
                row = act[at]
                prev = jnp.where(place == 0, before[f : f + 1], pltpu.roll(row, 1, 0))
                nxt = jnp.where(
                    place == frames - 1, after[f : f + 1], pltpu.roll(row, frames - 1, 0)
                )
                at = slice(f * frames, (f + 1) * frames)
                act3[at, 0:chans] = prev.astype(jnp.bfloat16)
                act3[at, chans : 2 * chans] = row.astype(jnp.bfloat16)
                act3[at, 2 * chans : 3 * chans] = nxt.astype(jnp.bfloat16)
            for i in taps:
                used = [f for f in range(rows_f) if 0 <= f - i + 1 < rows_f]
                span = slice(used[0] * frames, (used[-1] + 1) * frames)
                product = jnp.dot(act3[span], w[layer, i], preferred_element_type=jnp.float32)
                for k, f in enumerate(used):
                    add(f - i + 1, product[k * frames : (k + 1) * frames])
        hidden = jnp.concatenate(sums, axis=0)
        hmid[m] = hidden
        staged[m] = hidden.astype(jnp.bfloat16)

    def block_copy(m, begin, end, piece):
        span = pl.ds(begin * frames, (end - begin) * frames)
        return pltpu.make_async_remote_copy(
            src_ref=staged.at[m, span],
            dst_ref=xin.at[m, span],
            send_sem=blk_ssem.at[m],
            recv_sem=blk_rsem.at[m, piece],
            device_id=(up, tm),
            device_id_type=MESH,
        )

    ahead = jnp.where(first, min(FIRST, micros), min(2, micros))

    def step(k, carry):
        past = jnp.maximum(k - ahead, 0)
        rest = micros - ahead
        filling = k < ahead
        mixing = past < 2 * rest
        odd = lax.rem(past, 2) == 1
        entering = jnp.logical_or(filling, jnp.logical_and(mixing, odd))
        m = jnp.where(mixing, jnp.where(odd, ahead + past // 2, past // 2), past - rest)
        m = jnp.where(filling, k, m)
        landing = jnp.logical_and(entering, jnp.logical_not(first))
        stay = jnp.logical_and(entering, deep)
        rises = jnp.logical_not(jnp.logical_or(stay, last))
        layer = jnp.where(entering, 0, 1)

        @pl.when(landing)
        def _():
            await_letters(let_rsem.at[m, 0], 1)
            stats = unpack(jnp.sum(box[m, 0, :, edge_rows], axis=0))

            def load(low, high):
                landed = xin.at[m, pl.ds(low * frames, (high - low) * frames)]
                pltpu.make_async_copy(landed, landed, blk_rsem.at[m, 1 if low else 0]).wait()
                span = slice(low * frames, high * frames)
                return xin[m, span, :].astype(jnp.float32) + temb[pl.ds(m, 1), :]

            convolve(m, layer, stats, ((0, rows_f - 1, (0,)), (rows_f - 1, rows_f, (1, 2))), load)

        @pl.when(jnp.logical_or(stay, deep) & jnp.logical_not(landing))
        def _():
            @pl.when(jnp.logical_not(entering))
            def _():
                await_letters(let_rsem.at[m, 1], 0)

            stats = spread(
                [
                    jnp.sum(box[m, layer, :, edge_rows + k], axis=0)
                    for k in range(2 * halves)
                ]
            )
            convolve(
                m,
                layer,
                stats,
                ((0, rows_f, (0, 1, 2)),),
                lambda low, high: hmid[m, low * frames : high * frames, :],
            )

        @pl.when(stay)
        def _():
            summarize(m, 0, hmid[m])
            publish(m, 0, sec)

        @pl.when(jnp.logical_and(jnp.logical_or(entering, deep), rises))
        def _():
            block_copy(m, 0, LEAD, 0).start()
            summarize(m, 1, staged[m].astype(jnp.float32) + temb_next[pl.ds(m, 1), :])
            publish(m, 1, up)
            block_copy(m, LEAD, rows_f - 1, 0).start()
            block_copy(m, rows_f - 1, rows_f, 1).start()

        return carry

    for copy in small[:4]:
        copy.wait()
    half = chans // 2
    slots = temb.shape[0]
    which = lax.broadcasted_iota(jnp.int32, (slots, half), 0)
    steps_f = jnp.zeros((slots, half), jnp.float32)
    for m in range(micros):
        steps_f = jnp.where(which == m, timestep[m].astype(jnp.float32), steps_f)

    @pl.when(first)
    def _():
        level = jnp.cos(math.pi / 2.0 * (steps_f / STEPS + 0.008) / 1.008) ** 2
        keep = jnp.sqrt(level)
        blur = jnp.sqrt(1.0 - level)
        for copy in small[4:]:
            copy.wait()
        column = lax.broadcasted_iota(jnp.int32, (rows_f, 128), 1)
        for m in range(micros):
            mixed = keep[m : m + 1, 0:1] * clean[m] + blur[m : m + 1, 0:1] * noise[m]
            at = slice(m * rows_f, (m + 1) * rows_f)
            noisy[at, :] = mixed
            flat1 = jnp.sum(mixed, axis=1, keepdims=True)
            flat2 = jnp.sum(mixed * mixed, axis=1, keepdims=True)
            told[at, :] = jnp.where(
                column < 2,
                jnp.where(column == 0, flat1, flat2),
                jnp.where(column == 2, mixed[:, 0:1], mixed[:, frames - 1 : frames]),
            )

    order = lax.broadcasted_iota(jnp.int32, (slots, half), 1).astype(jnp.float32)
    angles = steps_f * jnp.exp(-math.log(10000.0) * order / half)
    temb[...] = jnp.dot(
        jnp.sin(angles).astype(jnp.bfloat16), proj[0:half, :], preferred_element_type=jnp.float32
    ) + jnp.dot(
        jnp.cos(angles).astype(jnp.bfloat16), proj[half:chans, :], preferred_element_type=jnp.float32
    )

    pl.semaphore_wait(barrier, n_time - 1 + n_time * jnp.where(first, 0, 1))

    def tell(peer):
        pltpu.make_async_remote_copy(
            src_ref=told,
            dst_ref=heard.at[tm],
            send_sem=heard_ssem,
            recv_sem=heard_rsem,
            device_id=(sec, peer),
            device_id_type=MESH,
        ).start()

    def invite(peer):
        pl.semaphore_signal(ready, inc=1, device_id=(down, peer), device_id_type=MESH)

    pass_temb = pltpu.make_async_remote_copy(
        src_ref=temb,
        dst_ref=temb_next,
        send_sem=temb_ssem,
        recv_sem=temb_rsem,
        device_id=(down, tm),
        device_id_type=MESH,
    )

    @pl.when(first)
    def _():
        each(1, n_time, tell)

    @pl.when(jnp.logical_not(first))
    def _():
        each(0, n_time, invite)
        pass_temb.start()

    load_w(0).wait()

    @pl.when(deep)
    def _():
        for layer in range(1, layers):
            load_w(layer).wait()

    @pl.when(first)
    def _():
        columns = jnp.transpose(noisy[...])
        for m in range(micros):
            for f in range(rows_f):
                at = m * rows_f + f
                hmid[m, f * frames : (f + 1) * frames, :] = (
                    columns[:, at : at + 1] * lift[...] + temb[m : m + 1, :]
                )
        heard[tm] = told[...]
        for m in range(micros):
            for k in range(2 * halves):
                box[m, 0, :, edge_rows + k] = jnp.zeros_like(box[m, 0, :, edge_rows + k])
        if n_time > 1:
            others = heard.at[pl.ds(0, n_time - 1)]
            pltpu.make_async_copy(others, others, heard_rsem).wait()
        total = jnp.sum(heard[...], axis=0)
        near = (heard[left][:, 3:4], heard[right][:, 2:3])
        for m in range(micros):
            at = slice(m * rows_f, (m + 1) * rows_f)
            flat = jnp.sum(total[at], axis=0, keepdims=True)
            shift = temb[m : m + 1, :]
            raised = lift[...] * flat[:, 0:1]
            both = (
                raised + positions * shift,
                lift[...] * (lift[...] * flat[:, 1:2])
                + 2.0 * shift * raised
                + positions * (shift * shift),
            )
            for v in range(2):
                for k in range(halves):
                    box[m, 0, 0, edge_rows + v * halves + k] = both[v][
                        :, k * 128 : (k + 1) * 128
                    ]
            for side, peer in ((0, left), (1, right)):
                edge = near[side][at] * lift[...] + shift
                for f in range(rows_f):
                    for k in range(halves):
                        box[m, 0, peer, k * rows_f + f] = edge[
                            f : f + 1, k * 128 : (k + 1) * 128
                        ]

    @pl.when(jnp.logical_not(last))
    def _():
        pltpu.make_async_copy(temb_next, temb_next, temb_rsem).wait()
        pl.semaphore_wait(ready, n_time)

    lax.fori_loop(0, 2 * micros, step, 0)

    @pl.when(first)
    def _():
        if n_time > 1:
            others = heard.at[pl.ds(0, n_time - 1)]
            pltpu.make_async_copy(others, others, heard_ssem).wait()

    @pl.when(jnp.logical_not(first))
    def _():
        pass_temb.wait_send()

    @pl.when(deep)
    def _():
        for m in range(micros):
            await_letters(let_ssem.at[m, 0], 0)

    @pl.when(jnp.logical_not(last))
    def _():
        for m in range(micros):
            await_letters(let_ssem.at[m, 1], 1)
            pltpu.make_async_copy(staged.at[m], staged.at[m], blk_ssem.at[m]).wait()


def on_device(clean, noise, timestep, lift, norm_gain, norm_bias, conv_weight, time_proj):
    n_time = lax.axis_size("tm")
    n_section = lax.axis_size("section")
    micros, rows_f, frames = clean.shape
    chans = lift.shape[0]
    layers = norm_gain.shape[1]
    slots = -(-micros // 8) * 8
    rows = rows_f * frames
    dims = (n_time, n_section, micros, rows_f, frames, chans, layers)
    letter_rows = (rows_f + 2) * (chans // 128)
    vmem = pl.BlockSpec(memory_space=pltpu.VMEM)
    hbm = pl.BlockSpec(memory_space=pl.ANY)
    dma = pltpu.SemaphoreType.DMA
    saved = pl.pallas_call(
        functools.partial(kernel, dims),
        out_shape=pltpu.VMEM((micros, rows, chans), jnp.bfloat16),
        in_specs=[hbm] * 8,
        out_specs=vmem,
        scratch_shapes=[
            pltpu.VMEM((layers, 3, 3 * chans, chans), jnp.bfloat16),
            pltpu.VMEM((micros, rows, chans), jnp.bfloat16),
            pltpu.VMEM((micros, rows, chans), jnp.float32),
            pltpu.VMEM((micros * rows_f, frames), jnp.float32),
            pltpu.VMEM((micros * rows_f, 128), jnp.float32),
            pltpu.VMEM((n_time, micros * rows_f, 128), jnp.float32),
            pltpu.VMEM((slots, chans), jnp.float32),
            pltpu.VMEM((micros, rows_f, frames), jnp.float32),
            pltpu.VMEM((micros, rows_f, frames), jnp.float32),
            pltpu.VMEM((1, chans), jnp.float32),
            pltpu.VMEM((layers, chans), jnp.float32),
            pltpu.VMEM((layers, chans), jnp.float32),
            pltpu.VMEM((chans, chans), jnp.bfloat16),
            pltpu.VMEM((slots, chans), jnp.float32),
            pltpu.SMEM((micros,), jnp.int32),
            pltpu.VMEM((rows, 3 * chans), jnp.bfloat16),
            pltpu.VMEM((micros, 2, 2, letter_rows, 1, 128), jnp.float32),
            pltpu.VMEM((micros, 2, n_time, letter_rows, 1, 128), jnp.float32),
            pltpu.VMEM((2 * (chans // 128) * n_time + 2 * letter_rows, 1, 128), jnp.float32),
            dma((micros, 2)),
            dma((micros, 2)),
            dma((micros,)),
            dma((micros, 2)),
            dma((layers,)),
            dma((7,)),
            dma,
            dma,
            dma,
            dma,
            pltpu.SemaphoreType.REGULAR,
        ],
        compiler_params=pltpu.CompilerParams(
            collective_id=0, has_side_effects=True, vmem_limit_bytes=48 * 2**20
        ),
    )(
        *(
            pltpu.with_memory_space_constraint(x, pltpu.HBM)
            for x in (
                timestep,
                clean,
                noise,
                lift.reshape(1, chans),
                norm_gain,
                norm_bias,
                time_proj,
                conv_weight.reshape(layers, 3, 3 * chans, chans),
            )
        ),
    )
    return saved.reshape(1, micros, rows_f, frames, chans)


def solution(mesh):
    in_specs = (
        P(None, None, "tm"),
        P(None, None, "tm"),
        P(),
        P(),
        P("section", None, None),
        P("section", None, None),
        P("section", None, None, None, None, None),
        P("section", None, None),
    )
    out_specs = P("section", None, None, "tm", None)
    return jax.shard_map(
        on_device, mesh=mesh, in_specs=in_specs, out_specs=out_specs, check_vma=False
    )
```

```python
import functools
import math

import jax
import jax.numpy as jnp
from jax import lax
from jax.experimental import pallas as pl
from jax.experimental.pallas import tpu as pltpu
from jax.sharding import PartitionSpec as P

GROUPS = 32
STEPS = 1000
LEAD = 1
FIRST = 3
MESH = pl.DeviceIdType.MESH


def silu(half):
    return half + half * jnp.tanh(half)


def kernel(
    dims,
    steps_in,
    clean_in,
    noise_in,
    lift_in,
    gains_in,
    biases_in,
    proj_in,
    weights,
    staged,
    w,
    xin,
    hmid,
    noisy,
    told,
    heard,
    temb_next,
    clean,
    noise,
    lift,
    gains,
    biases,
    proj,
    temb,
    timestep,
    act3,
    letter,
    box,
    tally,
    let_ssem,
    let_rsem,
    blk_ssem,
    blk_rsem,
    w_sem,
    in_sem,
    heard_ssem,
    heard_rsem,
    temb_ssem,
    temb_rsem,
    ready,
):
    n_time, n_section, micros, rows_f, frames, chans, layers = dims
    rows = rows_f * frames
    positions = rows * n_time
    width = chans // GROUPS
    count = positions * width
    halves = chans // 128
    edge_rows = rows_f * halves
    sec = lax.axis_index("section")
    tm = lax.axis_index("tm")
    deep = sec < n_section // 2
    first = sec == 0
    last = sec == n_section - 1
    has_left = tm > 0
    has_right = tm < n_time - 1
    left = jnp.maximum(tm - 1, 0)
    right = jnp.minimum(tm + 1, n_time - 1)
    up = jnp.minimum(sec + 1, n_section - 1)
    down = jnp.maximum(sec - 1, 0)
    short = n_time <= 8

    def each(begin, end, one):
        def step(r, carry):
            one(lax.rem(tm + r, n_time))
            return carry

        lax.fori_loop(begin, end, step, 0, unroll=short)

    def load_w(layer):
        return pltpu.make_async_copy(weights.at[layer], w.at[layer], w_sem.at[layer])

    small = [
        pltpu.make_async_copy(src, dst, in_sem.at[k])
        for k, (src, dst) in enumerate(
            [
                (steps_in, timestep),
                (proj_in.at[0], proj),
                (gains_in.at[0], gains),
                (biases_in.at[0], biases),
                (clean_in, clean),
                (noise_in, noise),
                (lift_in, lift),
            ]
        )
    ]

    barrier = pltpu.get_barrier_semaphore()

    def greet(section):
        def one(peer):
            pl.semaphore_signal(
                barrier, inc=1, device_id=(section, peer), device_id_type=MESH
            )

        return one

    each(1, n_time, greet(sec))

    for copy in small[:4]:
        copy.start()

    @pl.when(first)
    def _():
        for copy in small[4:]:
            copy.start()

    @pl.when(jnp.logical_not(last))
    def _():
        each(0, n_time, greet(up))

    load_w(0).start()

    @pl.when(deep)
    def _():
        for layer in range(1, layers):
            load_w(layer).start()

    lanes = lax.broadcasted_iota(jnp.int32, (8, 128), 1)
    tiers = lax.broadcasted_iota(jnp.int32, (8, 128), 0)
    spot = lanes % width
    quad = lanes % 4

    def turn(value, step):
        return value if step == 0 else pltpu.roll(value, step % 128, 1)

    def group_total(tall):
        total = tall
        for r in range(1, width):
            total = total + jnp.where(spot < width - r, turn(tall, -r), turn(tall, width - r))
        return total

    def pack(s1, s2):
        tall = jnp.where(
            tiers < 2,
            jnp.where(tiers == 0, s1[:, 0:128], s1[:, 128:256]),
            jnp.where(tiers == 2, s2[:, 0:128], s2[:, 128:256]),
        )
        total = group_total(tall)
        return jnp.sum(jnp.where(tiers == quad, total, 0.0), axis=0, keepdims=True)

    def spread(stats):
        tall = jnp.where(
            tiers < 2,
            jnp.where(tiers == 0, stats[0], stats[1]),
            jnp.where(tiers == 2, stats[2], stats[3]),
        )
        total = group_total(tall)
        return [total[k : k + 1] for k in range(2 * halves)]

    def unpack(packed):
        wide = jnp.broadcast_to(packed, (8, 128))
        turned = {k: turn(wide, k) for k in range(-3, 4)}
        found = []
        for v in range(4):
            low = jnp.where(quad == 0, turned[-v], turned[1 - v])
            high = jnp.where(quad == 2, turned[2 - v], turned[3 - v])
            found.append(jnp.where(quad < 2, low, high)[0:1])
        return found

    def summarize(m, kind, value):
        s1 = jnp.sum(value, axis=0, keepdims=True)
        s2 = jnp.sum(value * value, axis=0, keepdims=True)
        if kind:
            stats = [pack(s1, s2)]
        else:
            stats = [v[:, k * 128 : (k + 1) * 128] for v in (s1, s2) for k in range(halves)]
        for side in range(2):
            for f in range(rows_f):
                at = f * frames + side * (frames - 1)
                for k in range(halves):
                    letter[m, kind, side, k * rows_f + f] = value[
                        at : at + 1, k * 128 : (k + 1) * 128
                    ]
            for k, stat in enumerate(stats):
                letter[m, kind, side, edge_rows + k] = stat

    def post(m, kind, side, begin, rows_sent, section, peer):
        pltpu.make_async_remote_copy(
            src_ref=letter.at[m, kind, side, pl.ds(begin, rows_sent)],
            dst_ref=box.at[m, 1 - kind, tm, pl.ds(begin, rows_sent)],
            send_sem=let_ssem.at[m, kind],
            recv_sem=let_rsem.at[m, 1 - kind],
            device_id=(section, peer),
            device_id_type=MESH,
        ).start()

    stat_rows = (2 * halves, 1)

    def publish(m, kind, section):
        span = stat_rows[kind]

        def plain(peer):
            post(m, kind, 0, edge_rows, span, section, peer)

        each(2, n_time - 1, plain)

        @pl.when(has_right)
        def _():
            post(m, kind, 1, 0, edge_rows + span, section, right)

        @pl.when(has_left)
        def _():
            post(m, kind, 0, 0, edge_rows + span, section, left)

        if n_time > 2:

            @pl.when(jnp.logical_not(has_right))
            def _():
                plain(0)

            @pl.when(jnp.logical_not(has_left))
            def _():
                plain(n_time - 1)

        if kind:
            plain(tm)
        else:
            for k in range(span):
                box[m, 1, tm, edge_rows + k] = letter[m, 0, 0, edge_rows + k]

    def await_letters(sem, kind):
        plain = (n_time if kind else n_time - 1) * stat_rows[kind]

        def take(long):
            whole = tally.at[pl.ds(0, plain + long * edge_rows)]
            pltpu.make_async_copy(whole, whole, sem).wait()

        if n_time > 2:
            both = jnp.logical_and(has_left, has_right)

            @pl.when(both)
            def _():
                take(2)

            @pl.when(jnp.logical_not(both))
            def _():
                take(1)

        elif n_time == 2:
            take(1)
        elif plain:
            take(0)

    def convolve(m, layer, stats, stages, load):
        low1, high1, low2, high2 = stats
        gain = gains[pl.ds(layer, 1), :]
        bias = biases[pl.ds(layer, 1), :]
        scales, offsets = [], []
        for k, (s1, s2) in enumerate([(low1, low2), (high1, high2)]):
            at = slice(k * 128, (k + 1) * 128)
            mean = s1 / count
            var = jnp.maximum(s2 / count - mean * mean, 0.0)
            scale = lax.rsqrt(var + 1e-05) * (0.5 * gain[:, at])
            scales.append(scale)
            offsets.append(0.5 * bias[:, at] - mean * scale)
        scale = jnp.concatenate(scales, axis=1)
        offset = jnp.concatenate(offsets, axis=1)
        beyond = []
        for near, there in ((left, has_left), (right, has_right)):
            tall = jnp.concatenate([box[m, layer, near, r] for r in range(edge_rows)], axis=0)
            parts = [
                silu(tall[k * rows_f : (k + 1) * rows_f] * scales[k] + offsets[k])
                for k in range(halves)
            ]
            beyond.append(jnp.where(there, jnp.concatenate(parts, axis=1), 0.0))
        before, after = beyond
        place = lax.broadcasted_iota(jnp.int32, (frames, chans), 0)
        sums = [None] * rows_f

        def add(f, value):
            sums[f] = value if sums[f] is None else sums[f] + value

        for low, high, taps in stages:
            hidden = load(low, high)
            act = silu(hidden * scale + offset)
            for f in range(low, high):
                at = slice((f - low) * frames, (f - low + 1) * frames)
                add(f, hidden[at])
                row = act[at]
                prev = jnp.where(place == 0, before[f : f + 1], pltpu.roll(row, 1, 0))
                nxt = jnp.where(
                    place == frames - 1, after[f : f + 1], pltpu.roll(row, frames - 1, 0)
                )
                at = slice(f * frames, (f + 1) * frames)
                act3[at, 0:chans] = prev.astype(jnp.bfloat16)
                act3[at, chans : 2 * chans] = row.astype(jnp.bfloat16)
                act3[at, 2 * chans : 3 * chans] = nxt.astype(jnp.bfloat16)
            for i in taps:
                used = [f for f in range(rows_f) if 0 <= f - i + 1 < rows_f]
                span = slice(used[0] * frames, (used[-1] + 1) * frames)
                product = jnp.dot(act3[span], w[layer, i], preferred_element_type=jnp.float32)
                for k, f in enumerate(used):
                    add(f - i + 1, product[k * frames : (k + 1) * frames])
        hidden = jnp.concatenate(sums, axis=0)
        hmid[m] = hidden
        staged[m] = hidden.astype(jnp.bfloat16)

    def block_copy(m, begin, end, piece):
        span = pl.ds(begin * frames, (end - begin) * frames)
        return pltpu.make_async_remote_copy(
            src_ref=staged.at[m, span],
            dst_ref=xin.at[m, span],
            send_sem=blk_ssem.at[m],
            recv_sem=blk_rsem.at[m, piece],
            device_id=(up, tm),
            device_id_type=MESH,
        )

    ahead = jnp.where(first, min(FIRST, micros), min(2, micros))

    def step(k, carry):
        past = jnp.maximum(k - ahead, 0)
        rest = micros - ahead
        filling = k < ahead
        mixing = past < 2 * rest
        odd = lax.rem(past, 2) == 1
        entering = jnp.logical_or(filling, jnp.logical_and(mixing, odd))
        m = jnp.where(mixing, jnp.where(odd, ahead + past // 2, past // 2), past - rest)
        m = jnp.where(filling, k, m)
        landing = jnp.logical_and(entering, jnp.logical_not(first))
        stay = jnp.logical_and(entering, deep)
        rises = jnp.logical_not(jnp.logical_or(stay, last))
        layer = jnp.where(entering, 0, 1)

        @pl.when(landing)
        def _():
            await_letters(let_rsem.at[m, 0], 1)
            stats = unpack(jnp.sum(box[m, 0, :, edge_rows], axis=0))

            def load(low, high):
                landed = xin.at[m, pl.ds(low * frames, (high - low) * frames)]
                pltpu.make_async_copy(landed, landed, blk_rsem.at[m, 1 if low else 0]).wait()
                span = slice(low * frames, high * frames)
                return xin[m, span, :].astype(jnp.float32) + temb[pl.ds(m, 1), :]

            convolve(m, layer, stats, ((0, rows_f - 1, (0,)), (rows_f - 1, rows_f, (1, 2))), load)

        @pl.when(jnp.logical_or(stay, deep) & jnp.logical_not(landing))
        def _():
            @pl.when(jnp.logical_not(entering))
            def _():
                await_letters(let_rsem.at[m, 1], 0)

            stats = spread(
                [
                    jnp.sum(box[m, layer, :, edge_rows + k], axis=0)
                    for k in range(2 * halves)
                ]
            )
            convolve(
                m,
                layer,
                stats,
                ((0, rows_f, (0, 1, 2)),),
                lambda low, high: hmid[m, low * frames : high * frames, :],
            )

        @pl.when(stay)
        def _():
            summarize(m, 0, hmid[m])
            publish(m, 0, sec)

        @pl.when(jnp.logical_and(jnp.logical_or(entering, deep), rises))
        def _():
            @pl.when(m == 0)
            def _():
                pl.semaphore_wait(ready, n_time)
                pltpu.make_async_copy(temb_next, temb_next, temb_rsem).wait()

            block_copy(m, 0, LEAD, 0).start()
            summarize(m, 1, staged[m].astype(jnp.float32) + temb_next[pl.ds(m, 1), :])
            publish(m, 1, up)
            block_copy(m, LEAD, rows_f - 1, 0).start()
            block_copy(m, rows_f - 1, rows_f, 1).start()

        return carry

    for copy in small[:4]:
        copy.wait()
    half = chans // 2
    slots = temb.shape[0]
    which = lax.broadcasted_iota(jnp.int32, (slots, half), 0)
    steps_f = jnp.zeros((slots, half), jnp.float32)
    for m in range(micros):
        steps_f = jnp.where(which == m, timestep[m].astype(jnp.float32), steps_f)

    @pl.when(first)
    def _():
        level = jnp.cos(math.pi / 2.0 * (steps_f / STEPS + 0.008) / 1.008) ** 2
        keep = jnp.sqrt(level)
        blur = jnp.sqrt(1.0 - level)
        for copy in small[4:]:
            copy.wait()
        column = lax.broadcasted_iota(jnp.int32, (rows_f, 128), 1)
        for m in range(micros):
            mixed = keep[m : m + 1, 0:1] * clean[m] + blur[m : m + 1, 0:1] * noise[m]
            at = slice(m * rows_f, (m + 1) * rows_f)
            noisy[at, :] = mixed
            flat1 = jnp.sum(mixed, axis=1, keepdims=True)
            flat2 = jnp.sum(mixed * mixed, axis=1, keepdims=True)
            told[at, :] = jnp.where(
                column < 2,
                jnp.where(column == 0, flat1, flat2),
                jnp.where(column == 2, mixed[:, 0:1], mixed[:, frames - 1 : frames]),
            )

    order = lax.broadcasted_iota(jnp.int32, (slots, half), 1).astype(jnp.float32)
    angles = steps_f * jnp.exp(-math.log(10000.0) * order / half)
    temb[...] = jnp.dot(
        jnp.sin(angles).astype(jnp.bfloat16), proj[0:half, :], preferred_element_type=jnp.float32
    ) + jnp.dot(
        jnp.cos(angles).astype(jnp.bfloat16), proj[half:chans, :], preferred_element_type=jnp.float32
    )

    pl.semaphore_wait(barrier, n_time - 1 + n_time * jnp.where(first, 0, 1))

    def tell(peer):
        pltpu.make_async_remote_copy(
            src_ref=told,
            dst_ref=heard.at[tm],
            send_sem=heard_ssem,
            recv_sem=heard_rsem,
            device_id=(sec, peer),
            device_id_type=MESH,
        ).start()

    def invite(peer):
        pl.semaphore_signal(ready, inc=1, device_id=(down, peer), device_id_type=MESH)

    pass_temb = pltpu.make_async_remote_copy(
        src_ref=temb,
        dst_ref=temb_next,
        send_sem=temb_ssem,
        recv_sem=temb_rsem,
        device_id=(down, tm),
        device_id_type=MESH,
    )

    @pl.when(first)
    def _():
        each(1, n_time, tell)

    @pl.when(jnp.logical_not(first))
    def _():
        each(0, n_time, invite)
        pass_temb.start()

    load_w(0).wait()

    @pl.when(deep)
    def _():
        for layer in range(1, layers):
            load_w(layer).wait()

    @pl.when(first)
    def _():
        columns = jnp.transpose(noisy[...])
        for m in range(micros):
            for f in range(rows_f):
                at = m * rows_f + f
                hmid[m, f * frames : (f + 1) * frames, :] = (
                    columns[:, at : at + 1] * lift[...] + temb[m : m + 1, :]
                )
        heard[tm] = told[...]
        for m in range(micros):
            for k in range(2 * halves):
                box[m, 0, :, edge_rows + k] = jnp.zeros_like(box[m, 0, :, edge_rows + k])
        if n_time > 1:
            others = heard.at[pl.ds(0, n_time - 1)]
            pltpu.make_async_copy(others, others, heard_rsem).wait()
        total = jnp.sum(heard[...], axis=0)
        near = (heard[left][:, 3:4], heard[right][:, 2:3])
        for m in range(micros):
            at = slice(m * rows_f, (m + 1) * rows_f)
            flat = jnp.sum(total[at], axis=0, keepdims=True)
            shift = temb[m : m + 1, :]
            center = flat[:, 0:1] / positions
            wide = jnp.maximum(flat[:, 1:2] / positions - center * center, 0.0)
            middle = lift[...] * center + shift
            both = (
                positions * middle,
                positions * (lift[...] * lift[...] * wide + middle * middle),
            )
            for v in range(2):
                for k in range(halves):
                    box[m, 0, 0, edge_rows + v * halves + k] = both[v][
                        :, k * 128 : (k + 1) * 128
                    ]
            for side, peer in ((0, left), (1, right)):
                edge = near[side][at] * lift[...] + shift
                for f in range(rows_f):
                    for k in range(halves):
                        box[m, 0, peer, k * rows_f + f] = edge[
                            f : f + 1, k * 128 : (k + 1) * 128
                        ]

    lax.fori_loop(0, 2 * micros, step, 0)

    @pl.when(first)
    def _():
        if n_time > 1:
            others = heard.at[pl.ds(0, n_time - 1)]
            pltpu.make_async_copy(others, others, heard_ssem).wait()

    @pl.when(jnp.logical_not(first))
    def _():
        pass_temb.wait_send()

    @pl.when(deep)
    def _():
        for m in range(micros):
            await_letters(let_ssem.at[m, 0], 0)

    @pl.when(jnp.logical_not(last))
    def _():
        for m in range(micros):
            await_letters(let_ssem.at[m, 1], 1)
            pltpu.make_async_copy(staged.at[m], staged.at[m], blk_ssem.at[m]).wait()


def on_device(clean, noise, timestep, lift, norm_gain, norm_bias, conv_weight, time_proj):
    n_time = lax.axis_size("tm")
    n_section = lax.axis_size("section")
    micros, rows_f, frames = clean.shape
    chans = lift.shape[0]
    layers = norm_gain.shape[1]
    slots = -(-micros // 8) * 8
    rows = rows_f * frames
    dims = (n_time, n_section, micros, rows_f, frames, chans, layers)
    letter_rows = (rows_f + 2) * (chans // 128)
    vmem = pl.BlockSpec(memory_space=pltpu.VMEM)
    hbm = pl.BlockSpec(memory_space=pl.ANY)
    dma = pltpu.SemaphoreType.DMA
    saved = pl.pallas_call(
        functools.partial(kernel, dims),
        out_shape=pltpu.VMEM((micros, rows, chans), jnp.bfloat16),
        in_specs=[hbm] * 8,
        out_specs=vmem,
        scratch_shapes=[
            pltpu.VMEM((layers, 3, 3 * chans, chans), jnp.bfloat16),
            pltpu.VMEM((micros, rows, chans), jnp.bfloat16),
            pltpu.VMEM((micros, rows, chans), jnp.float32),
            pltpu.VMEM((micros * rows_f, frames), jnp.float32),
            pltpu.VMEM((micros * rows_f, 128), jnp.float32),
            pltpu.VMEM((n_time, micros * rows_f, 128), jnp.float32),
            pltpu.VMEM((slots, chans), jnp.float32),
            pltpu.VMEM((micros, rows_f, frames), jnp.float32),
            pltpu.VMEM((micros, rows_f, frames), jnp.float32),
            pltpu.VMEM((1, chans), jnp.float32),
            pltpu.VMEM((layers, chans), jnp.float32),
            pltpu.VMEM((layers, chans), jnp.float32),
            pltpu.VMEM((chans, chans), jnp.bfloat16),
            pltpu.VMEM((slots, chans), jnp.float32),
            pltpu.SMEM((micros,), jnp.int32),
            pltpu.VMEM((rows, 3 * chans), jnp.bfloat16),
            pltpu.VMEM((micros, 2, 2, letter_rows, 1, 128), jnp.float32),
            pltpu.VMEM((micros, 2, n_time, letter_rows, 1, 128), jnp.float32),
            pltpu.VMEM((2 * (chans // 128) * n_time + 2 * letter_rows, 1, 128), jnp.float32),
            dma((micros, 2)),
            dma((micros, 2)),
            dma((micros,)),
            dma((micros, 2)),
            dma((layers,)),
            dma((7,)),
            dma,
            dma,
            dma,
            dma,
            pltpu.SemaphoreType.REGULAR,
        ],
        compiler_params=pltpu.CompilerParams(
            collective_id=0, has_side_effects=True, vmem_limit_bytes=48 * 2**20
        ),
    )(
        *(
            pltpu.with_memory_space_constraint(x, pltpu.HBM)
            for x in (
                timestep,
                clean,
                noise,
                lift.reshape(1, chans),
                norm_gain,
                norm_bias,
                time_proj,
                conv_weight.reshape(layers, 3, 3 * chans, chans),
            )
        ),
    )
    return saved.reshape(1, micros, rows_f, frames, chans)


def solution(mesh):
    in_specs = (
        P(None, None, "tm"),
        P(None, None, "tm"),
        P(),
        P(),
        P("section", None, None),
        P("section", None, None),
        P("section", None, None, None, None, None),
        P("section", None, None),
    )
    out_specs = P("section", None, None, "tm", None)
    return jax.shard_map(
        on_device, mesh=mesh, in_specs=in_specs, out_specs=out_specs, check_vma=False
    )
```

```python
import functools
import math

import jax
import jax.numpy as jnp
from jax import lax
from jax.experimental import pallas as pl
from jax.experimental.pallas import tpu as pltpu
from jax.sharding import PartitionSpec as P

GROUPS = 32
STEPS = 1000
LEAD = 1
FIRST = 3
MESH = pl.DeviceIdType.MESH


def silu(half):
    return half + half * jnp.tanh(half)


def kernel(
    dims,
    steps_in,
    clean_in,
    noise_in,
    lift_in,
    gains_in,
    biases_in,
    proj_in,
    weights,
    staged,
    w,
    xin,
    hmid,
    noisy,
    told,
    heard,
    temb_next,
    clean,
    noise,
    lift,
    gains,
    biases,
    proj,
    temb,
    timestep,
    act3,
    letter,
    box,
    tally,
    let_ssem,
    let_rsem,
    blk_ssem,
    blk_rsem,
    w_sem,
    in_sem,
    heard_ssem,
    heard_rsem,
    temb_ssem,
    temb_rsem,
    ready,
):
    n_time, n_section, micros, rows_f, frames, chans, layers = dims
    rows = rows_f * frames
    positions = rows * n_time
    width = chans // GROUPS
    count = positions * width
    halves = chans // 128
    edge_rows = rows_f * halves
    sec = lax.axis_index("section")
    tm = lax.axis_index("tm")
    deep = sec < n_section // 2
    first = sec == 0
    last = sec == n_section - 1
    has_left = tm > 0
    has_right = tm < n_time - 1
    left = jnp.maximum(tm - 1, 0)
    right = jnp.minimum(tm + 1, n_time - 1)
    up = jnp.minimum(sec + 1, n_section - 1)
    down = jnp.maximum(sec - 1, 0)
    short = n_time <= 8

    def each(begin, end, one):
        def step(r, carry):
            one(lax.rem(tm + r, n_time))
            return carry

        lax.fori_loop(begin, end, step, 0, unroll=short)

    def load_w(layer):
        return pltpu.make_async_copy(weights.at[layer], w.at[layer], w_sem.at[layer])

    small = [
        pltpu.make_async_copy(src, dst, in_sem.at[k])
        for k, (src, dst) in enumerate(
            [
                (steps_in, timestep),
                (proj_in.at[0], proj),
                (gains_in.at[0], gains),
                (biases_in.at[0], biases),
                (clean_in, clean),
                (noise_in, noise),
                (lift_in, lift),
            ]
        )
    ]

    barrier = pltpu.get_barrier_semaphore()

    def greet(section):
        def one(peer):
            pl.semaphore_signal(
                barrier, inc=1, device_id=(section, peer), device_id_type=MESH
            )

        return one

    each(1, n_time, greet(sec))

    for copy in small[:4]:
        copy.start()

    @pl.when(first)
    def _():
        for copy in small[4:]:
            copy.start()

    @pl.when(jnp.logical_not(last))
    def _():
        each(0, n_time, greet(up))

    load_w(0).start()

    @pl.when(deep)
    def _():
        for layer in range(1, layers):
            load_w(layer).start()

    lanes = lax.broadcasted_iota(jnp.int32, (8, 128), 1)
    tiers = lax.broadcasted_iota(jnp.int32, (8, 128), 0)
    spot = lanes % width
    quad = lanes % 4

    def turn(value, step):
        return value if step == 0 else pltpu.roll(value, step % 128, 1)

    def group_total(tall):
        total = tall
        for r in range(1, width):
            total = total + jnp.where(spot < width - r, turn(tall, -r), turn(tall, width - r))
        return total

    def pack(s1, s2):
        tall = jnp.where(
            tiers < 2,
            jnp.where(tiers == 0, s1[:, 0:128], s1[:, 128:256]),
            jnp.where(tiers == 2, s2[:, 0:128], s2[:, 128:256]),
        )
        total = group_total(tall)
        return jnp.sum(jnp.where(tiers == quad, total, 0.0), axis=0, keepdims=True)

    def spread(stats):
        tall = jnp.where(
            tiers < 2,
            jnp.where(tiers == 0, stats[0], stats[1]),
            jnp.where(tiers == 2, stats[2], stats[3]),
        )
        total = group_total(tall)
        return [total[k : k + 1] for k in range(2 * halves)]

    def unpack(packed):
        wide = jnp.broadcast_to(packed, (8, 128))
        turned = {k: turn(wide, k) for k in range(-3, 4)}
        found = []
        for v in range(4):
            low = jnp.where(quad == 0, turned[-v], turned[1 - v])
            high = jnp.where(quad == 2, turned[2 - v], turned[3 - v])
            found.append(jnp.where(quad < 2, low, high)[0:1])
        return found

    def summarize(m, kind, value):
        s1 = jnp.sum(value, axis=0, keepdims=True)
        s2 = jnp.sum(value * value, axis=0, keepdims=True)
        if kind:
            stats = [pack(s1, s2)]
        else:
            stats = [v[:, k * 128 : (k + 1) * 128] for v in (s1, s2) for k in range(halves)]
        for side in range(2):
            for f in range(rows_f):
                at = f * frames + side * (frames - 1)
                for k in range(halves):
                    letter[m, kind, side, k * rows_f + f] = value[
                        at : at + 1, k * 128 : (k + 1) * 128
                    ]
            for k, stat in enumerate(stats):
                letter[m, kind, side, edge_rows + k] = stat

    def post(m, kind, side, begin, rows_sent, section, peer):
        pltpu.make_async_remote_copy(
            src_ref=letter.at[m, kind, side, pl.ds(begin, rows_sent)],
            dst_ref=box.at[m, 1 - kind, tm, pl.ds(begin, rows_sent)],
            send_sem=let_ssem.at[m, kind],
            recv_sem=let_rsem.at[m, 1 - kind],
            device_id=(section, peer),
            device_id_type=MESH,
        ).start()

    stat_rows = (2 * halves, 1)

    def publish(m, kind, section):
        span = stat_rows[kind]

        def plain(peer):
            post(m, kind, 0, edge_rows, span, section, peer)

        each(2, n_time - 1, plain)

        @pl.when(has_right)
        def _():
            post(m, kind, 1, 0, edge_rows + span, section, right)

        @pl.when(has_left)
        def _():
            post(m, kind, 0, 0, edge_rows + span, section, left)

        if n_time > 2:

            @pl.when(jnp.logical_not(has_right))
            def _():
                plain(0)

            @pl.when(jnp.logical_not(has_left))
            def _():
                plain(n_time - 1)

        if kind:
            plain(tm)
        else:
            for k in range(span):
                box[m, 1, tm, edge_rows + k] = letter[m, 0, 0, edge_rows + k]

    def await_letters(sem, kind):
        plain = (n_time if kind else n_time - 1) * stat_rows[kind]

        def take(long):
            whole = tally.at[pl.ds(0, plain + long * edge_rows)]
            pltpu.make_async_copy(whole, whole, sem).wait()

        if n_time > 2:
            both = jnp.logical_and(has_left, has_right)

            @pl.when(both)
            def _():
                take(2)

            @pl.when(jnp.logical_not(both))
            def _():
                take(1)

        elif n_time == 2:
            take(1)
        elif plain:
            take(0)

    def convolve(m, layer, stats, stages, load):
        low1, high1, low2, high2 = stats
        gain = gains[pl.ds(layer, 1), :]
        bias = biases[pl.ds(layer, 1), :]
        scales, offsets = [], []
        for k, (s1, s2) in enumerate([(low1, low2), (high1, high2)]):
            at = slice(k * 128, (k + 1) * 128)
            mean = s1 / count
            var = jnp.maximum(s2 / count - mean * mean, 0.0)
            scale = lax.rsqrt(var + 1e-05) * (0.5 * gain[:, at])
            scales.append(scale)
            offsets.append(0.5 * bias[:, at] - mean * scale)
        scale = jnp.concatenate(scales, axis=1)
        offset = jnp.concatenate(offsets, axis=1)
        beyond = []
        for near, there in ((left, has_left), (right, has_right)):
            tall = jnp.concatenate([box[m, layer, near, r] for r in range(edge_rows)], axis=0)
            parts = [
                silu(tall[k * rows_f : (k + 1) * rows_f] * scales[k] + offsets[k])
                for k in range(halves)
            ]
            beyond.append(jnp.where(there, jnp.concatenate(parts, axis=1), 0.0))
        before, after = beyond
        place = lax.broadcasted_iota(jnp.int32, (frames, chans), 0)
        sums = [None] * rows_f

        def add(f, value):
            sums[f] = value if sums[f] is None else sums[f] + value

        for low, high, taps in stages:
            hidden = load(low, high)
            act = silu(hidden * scale + offset)
            for f in range(low, high):
                at = slice((f - low) * frames, (f - low + 1) * frames)
                add(f, hidden[at])
                row = act[at]
                prev = jnp.where(place == 0, before[f : f + 1], pltpu.roll(row, 1, 0))
                nxt = jnp.where(
                    place == frames - 1, after[f : f + 1], pltpu.roll(row, frames - 1, 0)
                )
                at = slice(f * frames, (f + 1) * frames)
                act3[at, 0:chans] = prev.astype(jnp.bfloat16)
                act3[at, chans : 2 * chans] = row.astype(jnp.bfloat16)
                act3[at, 2 * chans : 3 * chans] = nxt.astype(jnp.bfloat16)
            for i in taps:
                used = [f for f in range(rows_f) if 0 <= f - i + 1 < rows_f]
                span = slice(used[0] * frames, (used[-1] + 1) * frames)
                product = jnp.dot(act3[span], w[layer, i], preferred_element_type=jnp.float32)
                for k, f in enumerate(used):
                    add(f - i + 1, product[k * frames : (k + 1) * frames])
        hidden = jnp.concatenate(sums, axis=0)
        hmid[m] = hidden
        staged[m] = hidden.astype(jnp.bfloat16)

    def block_copy(m, begin, end, piece):
        span = pl.ds(begin * frames, (end - begin) * frames)
        return pltpu.make_async_remote_copy(
            src_ref=staged.at[m, span],
            dst_ref=xin.at[m, span],
            send_sem=blk_ssem.at[m],
            recv_sem=blk_rsem.at[m, piece],
            device_id=(up, tm),
            device_id_type=MESH,
        )

    ahead = jnp.where(first, min(FIRST, micros), min(2, micros))

    def step(k, carry):
        past = jnp.maximum(k - ahead, 0)
        rest = micros - ahead
        filling = k < ahead
        mixing = past < 2 * rest
        odd = lax.rem(past, 2) == 1
        entering = jnp.logical_or(filling, jnp.logical_and(mixing, odd))
        m = jnp.where(mixing, jnp.where(odd, ahead + past // 2, past // 2), past - rest)
        m = jnp.where(filling, k, m)
        landing = jnp.logical_and(entering, jnp.logical_not(first))
        stay = jnp.logical_and(entering, deep)
        rises = jnp.logical_not(jnp.logical_or(stay, last))
        layer = jnp.where(entering, 0, 1)

        @pl.when(landing)
        def _():
            await_letters(let_rsem.at[m, 0], 1)
            stats = unpack(jnp.sum(box[m, 0, :, edge_rows], axis=0))

            def load(low, high):
                landed = xin.at[m, pl.ds(low * frames, (high - low) * frames)]
                pltpu.make_async_copy(landed, landed, blk_rsem.at[m, 1 if low else 0]).wait()
                span = slice(low * frames, high * frames)
                return xin[m, span, :].astype(jnp.float32) + temb[pl.ds(m, 1), :]

            convolve(m, layer, stats, ((0, rows_f - 1, (0,)), (rows_f - 1, rows_f, (1, 2))), load)

        @pl.when(jnp.logical_or(stay, deep) & jnp.logical_not(landing))
        def _():
            @pl.when(jnp.logical_not(entering))
            def _():
                await_letters(let_rsem.at[m, 1], 0)

            stats = spread(
                [
                    jnp.sum(box[m, layer, :, edge_rows + k], axis=0)
                    for k in range(2 * halves)
                ]
            )
            convolve(
                m,
                layer,
                stats,
                ((0, rows_f, (0, 1, 2)),),
                lambda low, high: hmid[m, low * frames : high * frames, :],
            )

        @pl.when(stay)
        def _():
            summarize(m, 0, hmid[m])
            publish(m, 0, sec)

        @pl.when(jnp.logical_and(jnp.logical_or(entering, deep), rises))
        def _():
            @pl.when(m == 0)
            def _():
                pl.semaphore_wait(ready, n_time)
                pltpu.make_async_copy(temb_next, temb_next, temb_rsem).wait()

            block_copy(m, 0, LEAD, 0).start()
            summarize(m, 1, staged[m].astype(jnp.float32) + temb_next[pl.ds(m, 1), :])
            publish(m, 1, up)
            block_copy(m, LEAD, rows_f - 1, 0).start()
            block_copy(m, rows_f - 1, rows_f, 1).start()

        return carry

    for copy in small[:4]:
        copy.wait()
    half = chans // 2
    slots = temb.shape[0]
    which = lax.broadcasted_iota(jnp.int32, (slots, half), 0)
    steps_f = jnp.zeros((slots, half), jnp.float32)
    for m in range(micros):
        steps_f = jnp.where(which == m, timestep[m].astype(jnp.float32), steps_f)

    @pl.when(first)
    def _():
        level = jnp.cos(math.pi / 2.0 * (steps_f / STEPS + 0.008) / 1.008) ** 2
        keep = jnp.sqrt(level)
        blur = jnp.sqrt(1.0 - level)
        for copy in small[4:]:
            copy.wait()
        lane = lax.broadcasted_iota(jnp.int32, (1, 128), 1)
        tallies = jnp.zeros((1, 128), jnp.float32)
        for m in range(micros):
            mixed = keep[m : m + 1, 0:1] * clean[m] + blur[m : m + 1, 0:1] * noise[m]
            noisy[m * rows_f : (m + 1) * rows_f, :] = mixed
            for k, value in enumerate((mixed, mixed * mixed)):
                flat = jnp.sum(jnp.sum(value, axis=0, keepdims=True), axis=1, keepdims=True)
                tallies = jnp.where(lane == k * micros + m, flat, tallies)
        told[0] = tallies
        columns = jnp.transpose(noisy[...])
        told[1, :, 0 : micros * rows_f] = columns[0:1, :]
        told[2, :, 0 : micros * rows_f] = columns[frames - 1 : frames, :]

    order = lax.broadcasted_iota(jnp.int32, (slots, half), 1).astype(jnp.float32)
    angles = steps_f * jnp.exp(-math.log(10000.0) * order / half)
    temb[...] = jnp.dot(
        jnp.sin(angles).astype(jnp.bfloat16), proj[0:half, :], preferred_element_type=jnp.float32
    ) + jnp.dot(
        jnp.cos(angles).astype(jnp.bfloat16), proj[half:chans, :], preferred_element_type=jnp.float32
    )

    pl.semaphore_wait(barrier, n_time - 1 + n_time * jnp.where(first, 0, 1))

    def tell(peer):
        pltpu.make_async_remote_copy(
            src_ref=told,
            dst_ref=heard.at[tm],
            send_sem=heard_ssem,
            recv_sem=heard_rsem,
            device_id=(sec, peer),
            device_id_type=MESH,
        ).start()

    def invite(peer):
        pl.semaphore_signal(ready, inc=1, device_id=(down, peer), device_id_type=MESH)

    pass_temb = pltpu.make_async_remote_copy(
        src_ref=temb,
        dst_ref=temb_next,
        send_sem=temb_ssem,
        recv_sem=temb_rsem,
        device_id=(down, tm),
        device_id_type=MESH,
    )

    @pl.when(first)
    def _():
        each(1, n_time, tell)

    @pl.when(jnp.logical_not(first))
    def _():
        each(0, n_time, invite)
        pass_temb.start()

    load_w(0).wait()

    @pl.when(deep)
    def _():
        for layer in range(1, layers):
            load_w(layer).wait()

    @pl.when(first)
    def _():
        columns = jnp.transpose(noisy[...])
        for m in range(micros):
            for f in range(rows_f):
                at = m * rows_f + f
                hmid[m, f * frames : (f + 1) * frames, :] = (
                    columns[:, at : at + 1] * lift[...] + temb[m : m + 1, :]
                )
        heard[tm] = told[...]
        for m in range(micros):
            for k in range(2 * halves):
                box[m, 0, :, edge_rows + k] = jnp.zeros_like(box[m, 0, :, edge_rows + k])
        if n_time > 1:
            others = heard.at[pl.ds(0, n_time - 1)]
            pltpu.make_async_copy(others, others, heard_rsem).wait()
        total = jnp.sum(heard[:, 0], axis=0)
        near = (heard[left, 2], heard[right, 1])
        for m in range(micros):
            shift = temb[m : m + 1, :]
            center = total[:, m : m + 1] / positions
            wide = jnp.maximum(
                total[:, micros + m : micros + m + 1] / positions - center * center, 0.0
            )
            middle = lift[...] * center + shift
            both = (
                positions * middle,
                positions * (lift[...] * lift[...] * wide + middle * middle),
            )
            for v in range(2):
                for k in range(halves):
                    box[m, 0, 0, edge_rows + v * halves + k] = both[v][
                        :, k * 128 : (k + 1) * 128
                    ]
            for side, peer in ((0, left), (1, right)):
                for f in range(rows_f):
                    at = m * rows_f + f
                    edge = near[side][:, at : at + 1] * lift[...] + shift
                    for k in range(halves):
                        box[m, 0, peer, k * rows_f + f] = edge[:, k * 128 : (k + 1) * 128]

    lax.fori_loop(0, 2 * micros, step, 0)

    @pl.when(first)
    def _():
        if n_time > 1:
            others = heard.at[pl.ds(0, n_time - 1)]
            pltpu.make_async_copy(others, others, heard_ssem).wait()

    @pl.when(jnp.logical_not(first))
    def _():
        pass_temb.wait_send()

    @pl.when(deep)
    def _():
        for m in range(micros):
            await_letters(let_ssem.at[m, 0], 0)

    @pl.when(jnp.logical_not(last))
    def _():
        for m in range(micros):
            await_letters(let_ssem.at[m, 1], 1)
            pltpu.make_async_copy(staged.at[m], staged.at[m], blk_ssem.at[m]).wait()


def on_device(clean, noise, timestep, lift, norm_gain, norm_bias, conv_weight, time_proj):
    n_time = lax.axis_size("tm")
    n_section = lax.axis_size("section")
    micros, rows_f, frames = clean.shape
    chans = lift.shape[0]
    layers = norm_gain.shape[1]
    slots = -(-micros // 8) * 8
    rows = rows_f * frames
    dims = (n_time, n_section, micros, rows_f, frames, chans, layers)
    letter_rows = (rows_f + 2) * (chans // 128)
    vmem = pl.BlockSpec(memory_space=pltpu.VMEM)
    hbm = pl.BlockSpec(memory_space=pl.ANY)
    dma = pltpu.SemaphoreType.DMA
    saved = pl.pallas_call(
        functools.partial(kernel, dims),
        out_shape=pltpu.VMEM((micros, rows, chans), jnp.bfloat16),
        in_specs=[hbm] * 8,
        out_specs=vmem,
        scratch_shapes=[
            pltpu.VMEM((layers, 3, 3 * chans, chans), jnp.bfloat16),
            pltpu.VMEM((micros, rows, chans), jnp.bfloat16),
            pltpu.VMEM((micros, rows, chans), jnp.float32),
            pltpu.VMEM((micros * rows_f, frames), jnp.float32),
            pltpu.VMEM((3, 1, 128), jnp.float32),
            pltpu.VMEM((n_time, 3, 1, 128), jnp.float32),
            pltpu.VMEM((slots, chans), jnp.float32),
            pltpu.VMEM((micros, rows_f, frames), jnp.float32),
            pltpu.VMEM((micros, rows_f, frames), jnp.float32),
            pltpu.VMEM((1, chans), jnp.float32),
            pltpu.VMEM((layers, chans), jnp.float32),
            pltpu.VMEM((layers, chans), jnp.float32),
            pltpu.VMEM((chans, chans), jnp.bfloat16),
            pltpu.VMEM((slots, chans), jnp.float32),
            pltpu.SMEM((micros,), jnp.int32),
            pltpu.VMEM((rows, 3 * chans), jnp.bfloat16),
            pltpu.VMEM((micros, 2, 2, letter_rows, 1, 128), jnp.float32),
            pltpu.VMEM((micros, 2, n_time, letter_rows, 1, 128), jnp.float32),
            pltpu.VMEM((2 * (chans // 128) * n_time + 2 * letter_rows, 1, 128), jnp.float32),
            dma((micros, 2)),
            dma((micros, 2)),
            dma((micros,)),
            dma((micros, 2)),
            dma((layers,)),
            dma((7,)),
            dma,
            dma,
            dma,
            dma,
            pltpu.SemaphoreType.REGULAR,
        ],
        compiler_params=pltpu.CompilerParams(
            collective_id=0, has_side_effects=True, vmem_limit_bytes=48 * 2**20
        ),
    )(
        *(
            pltpu.with_memory_space_constraint(x, pltpu.HBM)
            for x in (
                timestep,
                clean,
                noise,
                lift.reshape(1, chans),
                norm_gain,
                norm_bias,
                time_proj,
                conv_weight.reshape(layers, 3, 3 * chans, chans),
            )
        ),
    )
    return saved.reshape(1, micros, rows_f, frames, chans)


def solution(mesh):
    in_specs = (
        P(None, None, "tm"),
        P(None, None, "tm"),
        P(),
        P(),
        P("section", None, None),
        P("section", None, None),
        P("section", None, None, None, None, None),
        P("section", None, None),
    )
    out_specs = P("section", None, None, "tm", None)
    return jax.shard_map(
        on_device, mesh=mesh, in_specs=in_specs, out_specs=out_specs, check_vma=False
    )
```

```python
import functools
import math

import jax
import jax.numpy as jnp
from jax import lax
from jax.experimental import pallas as pl
from jax.experimental.pallas import tpu as pltpu
from jax.sharding import PartitionSpec as P

GROUPS = 32
STEPS = 1000
LEAD = 1
FIRST = 3
MESH = pl.DeviceIdType.MESH


def silu(half):
    return half + half * jnp.tanh(half)


def kernel(
    dims,
    steps_in,
    clean_in,
    noise_in,
    lift_in,
    gains_in,
    biases_in,
    proj_in,
    weights,
    staged,
    w,
    xin,
    hmid,
    noisy,
    told,
    heard,
    temb_next,
    clean,
    noise,
    lift,
    gains,
    biases,
    proj,
    temb,
    timestep,
    act3,
    letter,
    box,
    tally,
    let_ssem,
    let_rsem,
    blk_ssem,
    blk_rsem,
    w_sem,
    in_sem,
    heard_ssem,
    heard_rsem,
    temb_ssem,
    temb_rsem,
    ready,
):
    n_time, n_section, micros, rows_f, frames, chans, layers = dims
    rows = rows_f * frames
    positions = rows * n_time
    width = chans // GROUPS
    count = positions * width
    halves = chans // 128
    edge_rows = rows_f * halves
    sec = lax.axis_index("section")
    tm = lax.axis_index("tm")
    deep = sec < n_section // 2
    first = sec == 0
    last = sec == n_section - 1
    has_left = tm > 0
    has_right = tm < n_time - 1
    left = jnp.maximum(tm - 1, 0)
    right = jnp.minimum(tm + 1, n_time - 1)
    up = jnp.minimum(sec + 1, n_section - 1)
    down = jnp.maximum(sec - 1, 0)
    short = n_time <= 8

    def each(begin, end, one):
        def step(r, carry):
            one(lax.rem(tm + r, n_time))
            return carry

        lax.fori_loop(begin, end, step, 0, unroll=short)

    def load_w(layer):
        return pltpu.make_async_copy(weights.at[layer], w.at[layer], w_sem.at[layer])

    small = [
        pltpu.make_async_copy(src, dst, in_sem.at[k])
        for k, (src, dst) in enumerate(
            [
                (steps_in, timestep),
                (proj_in.at[0], proj),
                (gains_in.at[0], gains),
                (biases_in.at[0], biases),
                (clean_in, clean),
                (noise_in, noise),
                (lift_in, lift),
            ]
        )
    ]

    barrier = pltpu.get_barrier_semaphore()

    def greet(section):
        def one(peer):
            pl.semaphore_signal(
                barrier, inc=1, device_id=(section, peer), device_id_type=MESH
            )

        return one

    each(1, n_time, greet(sec))

    small[0].start()

    @pl.when(first)
    def _():
        for copy in small[4:]:
            copy.start()

    for copy in small[1:4]:
        copy.start()

    @pl.when(jnp.logical_not(last))
    def _():
        each(0, n_time, greet(up))

    load_w(0).start()

    @pl.when(deep)
    def _():
        for layer in range(1, layers):
            load_w(layer).start()

    lanes = lax.broadcasted_iota(jnp.int32, (8, 128), 1)
    tiers = lax.broadcasted_iota(jnp.int32, (8, 128), 0)
    spot = lanes % width
    quad = lanes % 4

    def turn(value, step):
        return value if step == 0 else pltpu.roll(value, step % 128, 1)

    def group_total(tall):
        total = tall
        for r in range(1, width):
            total = total + jnp.where(spot < width - r, turn(tall, -r), turn(tall, width - r))
        return total

    def pack(s1, s2):
        tall = jnp.where(
            tiers < 2,
            jnp.where(tiers == 0, s1[:, 0:128], s1[:, 128:256]),
            jnp.where(tiers == 2, s2[:, 0:128], s2[:, 128:256]),
        )
        total = group_total(tall)
        return jnp.sum(jnp.where(tiers == quad, total, 0.0), axis=0, keepdims=True)

    def spread(stats):
        tall = jnp.where(
            tiers < 2,
            jnp.where(tiers == 0, stats[0], stats[1]),
            jnp.where(tiers == 2, stats[2], stats[3]),
        )
        total = group_total(tall)
        return [total[k : k + 1] for k in range(2 * halves)]

    def unpack(packed):
        wide = jnp.broadcast_to(packed, (8, 128))
        turned = {k: turn(wide, k) for k in range(-3, 4)}
        found = []
        for v in range(4):
            low = jnp.where(quad == 0, turned[-v], turned[1 - v])
            high = jnp.where(quad == 2, turned[2 - v], turned[3 - v])
            found.append(jnp.where(quad < 2, low, high)[0:1])
        return found

    def summarize(m, kind, value):
        s1 = jnp.sum(value, axis=0, keepdims=True)
        s2 = jnp.sum(value * value, axis=0, keepdims=True)
        if kind:
            stats = [pack(s1, s2)]
        else:
            stats = [v[:, k * 128 : (k + 1) * 128] for v in (s1, s2) for k in range(halves)]
        for side in range(2):
            for f in range(rows_f):
                at = f * frames + side * (frames - 1)
                for k in range(halves):
                    letter[m, kind, side, k * rows_f + f] = value[
                        at : at + 1, k * 128 : (k + 1) * 128
                    ]
            for k, stat in enumerate(stats):
                letter[m, kind, side, edge_rows + k] = stat

    def post(m, kind, side, begin, rows_sent, section, peer):
        pltpu.make_async_remote_copy(
            src_ref=letter.at[m, kind, side, pl.ds(begin, rows_sent)],
            dst_ref=box.at[m, 1 - kind, tm, pl.ds(begin, rows_sent)],
            send_sem=let_ssem.at[m, kind],
            recv_sem=let_rsem.at[m, 1 - kind],
            device_id=(section, peer),
            device_id_type=MESH,
        ).start()

    stat_rows = (2 * halves, 1)

    def publish(m, kind, section):
        span = stat_rows[kind]

        def plain(peer):
            post(m, kind, 0, edge_rows, span, section, peer)

        @pl.when(has_right)
        def _():
            post(m, kind, 1, 0, edge_rows + span, section, right)

        @pl.when(has_left)
        def _():
            post(m, kind, 0, 0, edge_rows + span, section, left)

        if n_time > 2:

            @pl.when(jnp.logical_not(has_right))
            def _():
                plain(0)

            @pl.when(jnp.logical_not(has_left))
            def _():
                plain(n_time - 1)

        each(2, n_time - 1, plain)

        if kind:
            plain(tm)
        else:
            for k in range(span):
                box[m, 1, tm, edge_rows + k] = letter[m, 0, 0, edge_rows + k]

    def await_letters(sem, kind):
        plain = (n_time if kind else n_time - 1) * stat_rows[kind]

        def take(long):
            whole = tally.at[pl.ds(0, plain + long * edge_rows)]
            pltpu.make_async_copy(whole, whole, sem).wait()

        if n_time > 2:
            both = jnp.logical_and(has_left, has_right)

            @pl.when(both)
            def _():
                take(2)

            @pl.when(jnp.logical_not(both))
            def _():
                take(1)

        elif n_time == 2:
            take(1)
        elif plain:
            take(0)

    def convolve(m, layer, stats, stages, load):
        low1, high1, low2, high2 = stats
        gain = gains[pl.ds(layer, 1), :]
        bias = biases[pl.ds(layer, 1), :]
        scales, offsets = [], []
        for k, (s1, s2) in enumerate([(low1, low2), (high1, high2)]):
            at = slice(k * 128, (k + 1) * 128)
            mean = s1 / count
            var = jnp.maximum(s2 / count - mean * mean, 0.0)
            scale = lax.rsqrt(var + 1e-05) * (0.5 * gain[:, at])
            scales.append(scale)
            offsets.append(0.5 * bias[:, at] - mean * scale)
        scale = jnp.concatenate(scales, axis=1)
        offset = jnp.concatenate(offsets, axis=1)
        beyond = []
        for near, there in ((left, has_left), (right, has_right)):
            tall = jnp.concatenate([box[m, layer, near, r] for r in range(edge_rows)], axis=0)
            parts = [
                silu(tall[k * rows_f : (k + 1) * rows_f] * scales[k] + offsets[k])
                for k in range(halves)
            ]
            beyond.append(jnp.where(there, jnp.concatenate(parts, axis=1), 0.0))
        before, after = beyond
        place = lax.broadcasted_iota(jnp.int32, (frames, chans), 0)
        sums = [None] * rows_f

        def add(f, value):
            sums[f] = value if sums[f] is None else sums[f] + value

        for low, high, taps in stages:
            hidden = load(low, high)
            act = silu(hidden * scale + offset)
            for f in range(low, high):
                at = slice((f - low) * frames, (f - low + 1) * frames)
                add(f, hidden[at])
                row = act[at]
                prev = jnp.where(place == 0, before[f : f + 1], pltpu.roll(row, 1, 0))
                nxt = jnp.where(
                    place == frames - 1, after[f : f + 1], pltpu.roll(row, frames - 1, 0)
                )
                at = slice(f * frames, (f + 1) * frames)
                act3[at, 0:chans] = prev.astype(jnp.bfloat16)
                act3[at, chans : 2 * chans] = row.astype(jnp.bfloat16)
                act3[at, 2 * chans : 3 * chans] = nxt.astype(jnp.bfloat16)
            for i in taps:
                used = [f for f in range(rows_f) if 0 <= f - i + 1 < rows_f]
                span = slice(used[0] * frames, (used[-1] + 1) * frames)
                product = jnp.dot(act3[span], w[layer, i], preferred_element_type=jnp.float32)
                for k, f in enumerate(used):
                    add(f - i + 1, product[k * frames : (k + 1) * frames])
        hidden = jnp.concatenate(sums, axis=0)
        hmid[m] = hidden
        staged[m] = hidden.astype(jnp.bfloat16)

    def block_copy(m, begin, end, piece):
        span = pl.ds(begin * frames, (end - begin) * frames)
        return pltpu.make_async_remote_copy(
            src_ref=staged.at[m, span],
            dst_ref=xin.at[m, span],
            send_sem=blk_ssem.at[m],
            recv_sem=blk_rsem.at[m, piece],
            device_id=(up, tm),
            device_id_type=MESH,
        )

    ahead = jnp.where(first, min(FIRST, micros), min(2, micros))

    def step(k, carry):
        past = jnp.maximum(k - ahead, 0)
        rest = micros - ahead
        filling = k < ahead
        mixing = past < 2 * rest
        odd = lax.rem(past, 2) == 1
        entering = jnp.logical_or(filling, jnp.logical_and(mixing, odd))
        m = jnp.where(mixing, jnp.where(odd, ahead + past // 2, past // 2), past - rest)
        m = jnp.where(filling, k, m)
        landing = jnp.logical_and(entering, jnp.logical_not(first))
        stay = jnp.logical_and(entering, deep)
        rises = jnp.logical_not(jnp.logical_or(stay, last))
        layer = jnp.where(entering, 0, 1)

        @pl.when(landing)
        def _():
            await_letters(let_rsem.at[m, 0], 1)
            stats = unpack(jnp.sum(box[m, 0, :, edge_rows], axis=0))

            def load(low, high):
                landed = xin.at[m, pl.ds(low * frames, (high - low) * frames)]
                pltpu.make_async_copy(landed, landed, blk_rsem.at[m, 1 if low else 0]).wait()
                span = slice(low * frames, high * frames)
                return xin[m, span, :].astype(jnp.float32) + temb[pl.ds(m, 1), :]

            convolve(m, layer, stats, ((0, rows_f - 1, (0,)), (rows_f - 1, rows_f, (1, 2))), load)

        @pl.when(jnp.logical_or(stay, deep) & jnp.logical_not(landing))
        def _():
            @pl.when(jnp.logical_not(entering))
            def _():
                await_letters(let_rsem.at[m, 1], 0)

            stats = spread(
                [
                    jnp.sum(box[m, layer, :, edge_rows + k], axis=0)
                    for k in range(2 * halves)
                ]
            )
            convolve(
                m,
                layer,
                stats,
                ((0, rows_f, (0, 1, 2)),),
                lambda low, high: hmid[m, low * frames : high * frames, :],
            )

        @pl.when(stay)
        def _():
            summarize(m, 0, hmid[m])
            publish(m, 0, sec)

        @pl.when(jnp.logical_and(jnp.logical_or(entering, deep), rises))
        def _():
            @pl.when(m == 0)
            def _():
                pl.semaphore_wait(ready, n_time)
                pltpu.make_async_copy(temb_next, temb_next, temb_rsem).wait()

            block_copy(m, 0, LEAD, 0).start()
            summarize(m, 1, staged[m].astype(jnp.float32) + temb_next[pl.ds(m, 1), :])
            publish(m, 1, up)
            block_copy(m, LEAD, rows_f - 1, 0).start()
            block_copy(m, rows_f - 1, rows_f, 1).start()

        return carry

    small[0].wait()
    half = chans // 2
    slots = temb.shape[0]
    which = lax.broadcasted_iota(jnp.int32, (slots, half), 0)
    steps_f = jnp.zeros((slots, half), jnp.float32)
    for m in range(micros):
        steps_f = jnp.where(which == m, timestep[m].astype(jnp.float32), steps_f)

    @pl.when(first)
    def _():
        level = jnp.cos(math.pi / 2.0 * (steps_f / STEPS + 0.008) / 1.008) ** 2
        keep = jnp.sqrt(level)
        blur = jnp.sqrt(1.0 - level)
        for copy in small[4:]:
            copy.wait()
        lane = lax.broadcasted_iota(jnp.int32, (1, 128), 1)
        tallies = jnp.zeros((1, 128), jnp.float32)
        for m in range(micros):
            mixed = keep[m : m + 1, 0:1] * clean[m] + blur[m : m + 1, 0:1] * noise[m]
            noisy[m * rows_f : (m + 1) * rows_f, :] = mixed
            for k, value in enumerate((mixed, mixed * mixed)):
                flat = jnp.sum(jnp.sum(value, axis=0, keepdims=True), axis=1, keepdims=True)
                tallies = jnp.where(lane == k * micros + m, flat, tallies)
        told[0] = tallies
        columns = jnp.transpose(noisy[...])
        told[1, :, 0 : micros * rows_f] = columns[0:1, :]
        told[2, :, 0 : micros * rows_f] = columns[frames - 1 : frames, :]

    pl.semaphore_wait(barrier, n_time - 1 + n_time * jnp.where(first, 0, 1))

    def tell(peer):
        pltpu.make_async_remote_copy(
            src_ref=told,
            dst_ref=heard.at[tm],
            send_sem=heard_ssem,
            recv_sem=heard_rsem,
            device_id=(sec, peer),
            device_id_type=MESH,
        ).start()

    def invite(peer):
        pl.semaphore_signal(ready, inc=1, device_id=(down, peer), device_id_type=MESH)

    pass_temb = pltpu.make_async_remote_copy(
        src_ref=temb,
        dst_ref=temb_next,
        send_sem=temb_ssem,
        recv_sem=temb_rsem,
        device_id=(down, tm),
        device_id_type=MESH,
    )

    @pl.when(first)
    def _():
        each(1, n_time, tell)

    for copy in small[1:4]:
        copy.wait()
    order = lax.broadcasted_iota(jnp.int32, (slots, half), 1).astype(jnp.float32)
    angles = steps_f * jnp.exp(-math.log(10000.0) * order / half)
    temb[...] = jnp.dot(
        jnp.sin(angles).astype(jnp.bfloat16), proj[0:half, :], preferred_element_type=jnp.float32
    ) + jnp.dot(
        jnp.cos(angles).astype(jnp.bfloat16), proj[half:chans, :], preferred_element_type=jnp.float32
    )

    @pl.when(jnp.logical_not(first))
    def _():
        each(0, n_time, invite)
        pass_temb.start()

    load_w(0).wait()

    @pl.when(deep)
    def _():
        for layer in range(1, layers):
            load_w(layer).wait()

    @pl.when(first)
    def _():
        columns = jnp.transpose(noisy[...])
        for m in range(micros):
            for f in range(rows_f):
                at = m * rows_f + f
                hmid[m, f * frames : (f + 1) * frames, :] = (
                    columns[:, at : at + 1] * lift[...] + temb[m : m + 1, :]
                )
        heard[tm] = told[...]
        for m in range(micros):
            for k in range(2 * halves):
                box[m, 0, :, edge_rows + k] = jnp.zeros_like(box[m, 0, :, edge_rows + k])
        if n_time > 1:
            others = heard.at[pl.ds(0, n_time - 1)]
            pltpu.make_async_copy(others, others, heard_rsem).wait()
        total = jnp.sum(heard[:, 0], axis=0)
        near = (heard[left, 2], heard[right, 1])
        for m in range(micros):
            shift = temb[m : m + 1, :]
            center = total[:, m : m + 1] / positions
            wide = jnp.maximum(
                total[:, micros + m : micros + m + 1] / positions - center * center, 0.0
            )
            middle = lift[...] * center + shift
            both = (
                positions * middle,
                positions * (lift[...] * lift[...] * wide + middle * middle),
            )
            for v in range(2):
                for k in range(halves):
                    box[m, 0, 0, edge_rows + v * halves + k] = both[v][
                        :, k * 128 : (k + 1) * 128
                    ]
            for side, peer in ((0, left), (1, right)):
                for f in range(rows_f):
                    at = m * rows_f + f
                    edge = near[side][:, at : at + 1] * lift[...] + shift
                    for k in range(halves):
                        box[m, 0, peer, k * rows_f + f] = edge[:, k * 128 : (k + 1) * 128]

    lax.fori_loop(0, 2 * micros, step, 0)

    @pl.when(first)
    def _():
        if n_time > 1:
            others = heard.at[pl.ds(0, n_time - 1)]
            pltpu.make_async_copy(others, others, heard_ssem).wait()

    @pl.when(jnp.logical_not(first))
    def _():
        pass_temb.wait_send()

    @pl.when(deep)
    def _():
        for m in range(micros):
            await_letters(let_ssem.at[m, 0], 0)

    @pl.when(jnp.logical_not(last))
    def _():
        for m in range(micros):
            await_letters(let_ssem.at[m, 1], 1)
            pltpu.make_async_copy(staged.at[m], staged.at[m], blk_ssem.at[m]).wait()


def on_device(clean, noise, timestep, lift, norm_gain, norm_bias, conv_weight, time_proj):
    n_time = lax.axis_size("tm")
    n_section = lax.axis_size("section")
    micros, rows_f, frames = clean.shape
    chans = lift.shape[0]
    layers = norm_gain.shape[1]
    slots = -(-micros // 8) * 8
    rows = rows_f * frames
    dims = (n_time, n_section, micros, rows_f, frames, chans, layers)
    letter_rows = (rows_f + 2) * (chans // 128)
    vmem = pl.BlockSpec(memory_space=pltpu.VMEM)
    hbm = pl.BlockSpec(memory_space=pl.ANY)
    dma = pltpu.SemaphoreType.DMA
    saved = pl.pallas_call(
        functools.partial(kernel, dims),
        out_shape=pltpu.VMEM((micros, rows, chans), jnp.bfloat16),
        in_specs=[hbm] * 8,
        out_specs=vmem,
        scratch_shapes=[
            pltpu.VMEM((layers, 3, 3 * chans, chans), jnp.bfloat16),
            pltpu.VMEM((micros, rows, chans), jnp.bfloat16),
            pltpu.VMEM((micros, rows, chans), jnp.float32),
            pltpu.VMEM((micros * rows_f, frames), jnp.float32),
            pltpu.VMEM((3, 1, 128), jnp.float32),
            pltpu.VMEM((n_time, 3, 1, 128), jnp.float32),
            pltpu.VMEM((slots, chans), jnp.float32),
            pltpu.VMEM((micros, rows_f, frames), jnp.float32),
            pltpu.VMEM((micros, rows_f, frames), jnp.float32),
            pltpu.VMEM((1, chans), jnp.float32),
            pltpu.VMEM((layers, chans), jnp.float32),
            pltpu.VMEM((layers, chans), jnp.float32),
            pltpu.VMEM((chans, chans), jnp.bfloat16),
            pltpu.VMEM((slots, chans), jnp.float32),
            pltpu.SMEM((micros,), jnp.int32),
            pltpu.VMEM((rows, 3 * chans), jnp.bfloat16),
            pltpu.VMEM((micros, 2, 2, letter_rows, 1, 128), jnp.float32),
            pltpu.VMEM((micros, 2, n_time, letter_rows, 1, 128), jnp.float32),
            pltpu.VMEM((2 * (chans // 128) * n_time + 2 * letter_rows, 1, 128), jnp.float32),
            dma((micros, 2)),
            dma((micros, 2)),
            dma((micros,)),
            dma((micros, 2)),
            dma((layers,)),
            dma((7,)),
            dma,
            dma,
            dma,
            dma,
            pltpu.SemaphoreType.REGULAR,
        ],
        compiler_params=pltpu.CompilerParams(
            collective_id=0, has_side_effects=True, vmem_limit_bytes=48 * 2**20
        ),
    )(
        *(
            pltpu.with_memory_space_constraint(x, pltpu.HBM)
            for x in (
                timestep,
                clean,
                noise,
                lift.reshape(1, chans),
                norm_gain,
                norm_bias,
                time_proj,
                conv_weight.reshape(layers, 3, 3 * chans, chans),
            )
        ),
    )
    return saved.reshape(1, micros, rows_f, frames, chans)


def solution(mesh):
    in_specs = (
        P(None, None, "tm"),
        P(None, None, "tm"),
        P(),
        P(),
        P("section", None, None),
        P("section", None, None),
        P("section", None, None, None, None, None),
        P("section", None, None),
    )
    out_specs = P("section", None, None, "tm", None)
    return jax.shard_map(
        on_device, mesh=mesh, in_specs=in_specs, out_specs=out_specs, check_vma=False
    )
```

```python
import functools
import math

import jax
import jax.numpy as jnp
from jax import lax
from jax.experimental import pallas as pl
from jax.experimental.pallas import tpu as pltpu
from jax.sharding import PartitionSpec as P

GROUPS = 32
STEPS = 1000
LEAD = 3
MIDDLE = 5
FIRST = 3
MESH = pl.DeviceIdType.MESH


def silu(half):
    return half + half * jnp.tanh(half)


def kernel(
    dims,
    steps_in,
    clean_in,
    noise_in,
    lift_in,
    gains_in,
    biases_in,
    proj_in,
    weights,
    staged,
    w,
    xin,
    hmid,
    noisy,
    told,
    heard,
    temb_next,
    clean,
    noise,
    lift,
    gains,
    biases,
    proj,
    temb,
    timestep,
    act3,
    letter,
    box,
    tally,
    let_ssem,
    let_rsem,
    blk_ssem,
    blk_rsem,
    w_sem,
    in_sem,
    heard_ssem,
    heard_rsem,
    temb_ssem,
    temb_rsem,
    ready,
):
    n_time, n_section, micros, rows_f, frames, chans, layers = dims
    rows = rows_f * frames
    positions = rows * n_time
    width = chans // GROUPS
    count = positions * width
    halves = chans // 128
    edge_rows = rows_f * halves
    sec = lax.axis_index("section")
    tm = lax.axis_index("tm")
    deep = sec < n_section // 2
    first = sec == 0
    last = sec == n_section - 1
    has_left = tm > 0
    has_right = tm < n_time - 1
    left = jnp.maximum(tm - 1, 0)
    right = jnp.minimum(tm + 1, n_time - 1)
    up = jnp.minimum(sec + 1, n_section - 1)
    down = jnp.maximum(sec - 1, 0)
    short = n_time <= 8

    def each(begin, end, one):
        def step(r, carry):
            one(lax.rem(tm + r, n_time))
            return carry

        lax.fori_loop(begin, end, step, 0, unroll=short)

    def load_w(layer):
        return pltpu.make_async_copy(weights.at[layer], w.at[layer], w_sem.at[layer])

    small = [
        pltpu.make_async_copy(src, dst, in_sem.at[k])
        for k, (src, dst) in enumerate(
            [
                (steps_in, timestep),
                (proj_in.at[0], proj),
                (gains_in.at[0], gains),
                (biases_in.at[0], biases),
                (clean_in, clean),
                (noise_in, noise),
                (lift_in, lift),
            ]
        )
    ]

    barrier = pltpu.get_barrier_semaphore()

    def greet(section):
        def one(peer):
            pl.semaphore_signal(
                barrier, inc=1, device_id=(section, peer), device_id_type=MESH
            )

        return one

    each(1, n_time, greet(sec))

    small[0].start()

    @pl.when(first)
    def _():
        for copy in small[4:]:
            copy.start()

    for copy in small[1:4]:
        copy.start()

    @pl.when(jnp.logical_not(last))
    def _():
        each(0, n_time, greet(up))

    load_w(0).start()

    @pl.when(deep)
    def _():
        for layer in range(1, layers):
            load_w(layer).start()

    lanes = lax.broadcasted_iota(jnp.int32, (8, 128), 1)
    tiers = lax.broadcasted_iota(jnp.int32, (8, 128), 0)
    spot = lanes % width
    quad = lanes % 4

    def turn(value, step):
        return value if step == 0 else pltpu.roll(value, step % 128, 1)

    def group_total(tall):
        total = tall
        for r in range(1, width):
            total = total + jnp.where(spot < width - r, turn(tall, -r), turn(tall, width - r))
        return total

    def pack(s1, s2):
        tall = jnp.where(
            tiers < 2,
            jnp.where(tiers == 0, s1[:, 0:128], s1[:, 128:256]),
            jnp.where(tiers == 2, s2[:, 0:128], s2[:, 128:256]),
        )
        total = group_total(tall)
        return jnp.sum(jnp.where(tiers == quad, total, 0.0), axis=0, keepdims=True)

    def spread(stats):
        tall = jnp.where(
            tiers < 2,
            jnp.where(tiers == 0, stats[0], stats[1]),
            jnp.where(tiers == 2, stats[2], stats[3]),
        )
        total = group_total(tall)
        return [total[k : k + 1] for k in range(2 * halves)]

    def unpack(packed):
        wide = jnp.broadcast_to(packed, (8, 128))
        turned = {k: turn(wide, k) for k in range(-3, 4)}
        found = []
        for v in range(4):
            low = jnp.where(quad == 0, turned[-v], turned[1 - v])
            high = jnp.where(quad == 2, turned[2 - v], turned[3 - v])
            found.append(jnp.where(quad < 2, low, high)[0:1])
        return found

    def summarize(m, kind, value):
        s1 = jnp.sum(value, axis=0, keepdims=True)
        s2 = jnp.sum(value * value, axis=0, keepdims=True)
        if kind:
            stats = [pack(s1, s2)]
        else:
            stats = [v[:, k * 128 : (k + 1) * 128] for v in (s1, s2) for k in range(halves)]
        for side in range(2):
            for f in range(rows_f):
                at = f * frames + side * (frames - 1)
                for k in range(halves):
                    letter[m, kind, side, k * rows_f + f] = value[
                        at : at + 1, k * 128 : (k + 1) * 128
                    ]
            for k, stat in enumerate(stats):
                letter[m, kind, side, edge_rows + k] = stat

    def post(m, kind, side, begin, rows_sent, section, peer):
        pltpu.make_async_remote_copy(
            src_ref=letter.at[m, kind, side, pl.ds(begin, rows_sent)],
            dst_ref=box.at[m, 1 - kind, tm, pl.ds(begin, rows_sent)],
            send_sem=let_ssem.at[m, kind],
            recv_sem=let_rsem.at[m, 1 - kind],
            device_id=(section, peer),
            device_id_type=MESH,
        ).start()

    stat_rows = (2 * halves, 1)

    def publish(m, kind, section, between=None):
        span = stat_rows[kind]

        def plain(peer):
            post(m, kind, 0, edge_rows, span, section, peer)

        @pl.when(has_right)
        def _():
            post(m, kind, 1, 0, edge_rows + span, section, right)

        @pl.when(has_left)
        def _():
            post(m, kind, 0, 0, edge_rows + span, section, left)

        if n_time > 2:

            @pl.when(jnp.logical_not(has_right))
            def _():
                plain(0)

            @pl.when(jnp.logical_not(has_left))
            def _():
                plain(n_time - 1)

        each(2, max(n_time // 2, 2), plain)
        if between is not None:
            between()
        each(max(n_time // 2, 2), n_time - 1, plain)

        if kind:
            plain(tm)
        else:
            for k in range(span):
                box[m, 1, tm, edge_rows + k] = letter[m, 0, 0, edge_rows + k]

    def await_letters(sem, kind):
        plain = (n_time if kind else n_time - 1) * stat_rows[kind]

        def take(long):
            whole = tally.at[pl.ds(0, plain + long * edge_rows)]
            pltpu.make_async_copy(whole, whole, sem).wait()

        if n_time > 2:
            both = jnp.logical_and(has_left, has_right)

            @pl.when(both)
            def _():
                take(2)

            @pl.when(jnp.logical_not(both))
            def _():
                take(1)

        elif n_time == 2:
            take(1)
        elif plain:
            take(0)

    def convolve(m, layer, stats, stages, load):
        low1, high1, low2, high2 = stats
        gain = gains[pl.ds(layer, 1), :]
        bias = biases[pl.ds(layer, 1), :]
        scales, offsets = [], []
        for k, (s1, s2) in enumerate([(low1, low2), (high1, high2)]):
            at = slice(k * 128, (k + 1) * 128)
            mean = s1 / count
            var = jnp.maximum(s2 / count - mean * mean, 0.0)
            scale = lax.rsqrt(var + 1e-05) * (0.5 * gain[:, at])
            scales.append(scale)
            offsets.append(0.5 * bias[:, at] - mean * scale)
        scale = jnp.concatenate(scales, axis=1)
        offset = jnp.concatenate(offsets, axis=1)
        beyond = []
        for near, there in ((left, has_left), (right, has_right)):
            tall = jnp.concatenate([box[m, layer, near, r] for r in range(edge_rows)], axis=0)
            parts = [
                silu(tall[k * rows_f : (k + 1) * rows_f] * scales[k] + offsets[k])
                for k in range(halves)
            ]
            beyond.append(jnp.where(there, jnp.concatenate(parts, axis=1), 0.0))
        before, after = beyond
        place = lax.broadcasted_iota(jnp.int32, (frames, chans), 0)
        sums = [None] * rows_f

        def add(f, value):
            sums[f] = value if sums[f] is None else sums[f] + value

        for low, high, taps in stages:
            hidden = load(low, high)
            act = silu(hidden * scale + offset)
            for f in range(low, high):
                at = slice((f - low) * frames, (f - low + 1) * frames)
                add(f, hidden[at])
                row = act[at]
                prev = jnp.where(place == 0, before[f : f + 1], pltpu.roll(row, 1, 0))
                nxt = jnp.where(
                    place == frames - 1, after[f : f + 1], pltpu.roll(row, frames - 1, 0)
                )
                at = slice(f * frames, (f + 1) * frames)
                act3[at, 0:chans] = prev.astype(jnp.bfloat16)
                act3[at, chans : 2 * chans] = row.astype(jnp.bfloat16)
                act3[at, 2 * chans : 3 * chans] = nxt.astype(jnp.bfloat16)
            for i in taps:
                used = [f for f in range(rows_f) if 0 <= f - i + 1 < rows_f]
                span = slice(used[0] * frames, (used[-1] + 1) * frames)
                product = jnp.dot(act3[span], w[layer, i], preferred_element_type=jnp.float32)
                for k, f in enumerate(used):
                    add(f - i + 1, product[k * frames : (k + 1) * frames])
        hidden = jnp.concatenate(sums, axis=0)
        hmid[m] = hidden
        staged[m] = hidden.astype(jnp.bfloat16)

    def block_copy(m, begin, end, piece):
        span = pl.ds(begin, end - begin)
        return pltpu.make_async_remote_copy(
            src_ref=staged.at[m, span],
            dst_ref=xin.at[m, span],
            send_sem=blk_ssem.at[m],
            recv_sem=blk_rsem.at[m, piece],
            device_id=(up, tm),
            device_id_type=MESH,
        )

    ahead = jnp.where(first, min(FIRST, micros), min(2, micros))

    def step(k, carry):
        past = jnp.maximum(k - ahead, 0)
        rest = micros - ahead
        filling = k < ahead
        mixing = past < 2 * rest
        odd = lax.rem(past, 2) == 1
        entering = jnp.logical_or(filling, jnp.logical_and(mixing, odd))
        m = jnp.where(mixing, jnp.where(odd, ahead + past // 2, past // 2), past - rest)
        m = jnp.where(filling, k, m)
        landing = jnp.logical_and(entering, jnp.logical_not(first))
        stay = jnp.logical_and(entering, deep)
        rises = jnp.logical_not(jnp.logical_or(stay, last))
        layer = jnp.where(entering, 0, 1)

        @pl.when(landing)
        def _():
            await_letters(let_rsem.at[m, 0], 1)
            stats = unpack(jnp.sum(box[m, 0, :, edge_rows], axis=0))

            def load(low, high):
                landed = xin.at[m, pl.ds(low * frames, (high - low) * frames)]
                pltpu.make_async_copy(landed, landed, blk_rsem.at[m, 1 if low else 0]).wait()
                span = slice(low * frames, high * frames)
                return xin[m, span, :].astype(jnp.float32) + temb[pl.ds(m, 1), :]

            convolve(m, layer, stats, ((0, rows_f - 1, (0,)), (rows_f - 1, rows_f, (1, 2))), load)

        @pl.when(jnp.logical_or(stay, deep) & jnp.logical_not(landing))
        def _():
            @pl.when(jnp.logical_not(entering))
            def _():
                await_letters(let_rsem.at[m, 1], 0)

            stats = spread(
                [
                    jnp.sum(box[m, layer, :, edge_rows + k], axis=0)
                    for k in range(2 * halves)
                ]
            )
            convolve(
                m,
                layer,
                stats,
                ((0, rows_f, (0, 1, 2)),),
                lambda low, high: hmid[m, low * frames : high * frames, :],
            )

        @pl.when(stay)
        def _():
            summarize(m, 0, hmid[m])
            publish(m, 0, sec)

        @pl.when(jnp.logical_and(jnp.logical_or(entering, deep), rises))
        def _():
            @pl.when(m == 0)
            def _():
                pl.semaphore_wait(ready, n_time)
                pltpu.make_async_copy(temb_next, temb_next, temb_rsem).wait()

            block_copy(m, 0, LEAD * frames // 4, 0).start()
            summarize(m, 1, staged[m].astype(jnp.float32) + temb_next[pl.ds(m, 1), :])
            publish(
                m,
                1,
                up,
                lambda: block_copy(m, LEAD * frames // 4, MIDDLE * frames // 4, 0).start(),
            )
            block_copy(m, MIDDLE * frames // 4, (rows_f - 1) * frames, 0).start()
            block_copy(m, (rows_f - 1) * frames, rows, 1).start()

        return carry

    small[0].wait()
    half = chans // 2
    slots = temb.shape[0]
    which = lax.broadcasted_iota(jnp.int32, (slots, half), 0)
    steps_f = jnp.zeros((slots, half), jnp.float32)
    for m in range(micros):
        steps_f = jnp.where(which == m, timestep[m].astype(jnp.float32), steps_f)

    @pl.when(first)
    def _():
        level = jnp.cos(math.pi / 2.0 * (steps_f / STEPS + 0.008) / 1.008) ** 2
        keep = jnp.sqrt(level)
        blur = jnp.sqrt(1.0 - level)
        for copy in small[4:]:
            copy.wait()
        lane = lax.broadcasted_iota(jnp.int32, (1, 128), 1)
        tallies = jnp.zeros((1, 128), jnp.float32)
        for m in range(micros):
            mixed = keep[m : m + 1, 0:1] * clean[m] + blur[m : m + 1, 0:1] * noise[m]
            noisy[m * rows_f : (m + 1) * rows_f, :] = mixed
            for k, value in enumerate((mixed, mixed * mixed)):
                flat = jnp.sum(jnp.sum(value, axis=0, keepdims=True), axis=1, keepdims=True)
                tallies = jnp.where(lane == k * micros + m, flat, tallies)
        told[0] = tallies
        columns = jnp.transpose(noisy[...])
        told[1, :, 0 : micros * rows_f] = columns[0:1, :]
        told[2, :, 0 : micros * rows_f] = columns[frames - 1 : frames, :]

    pl.semaphore_wait(barrier, n_time - 1 + n_time * jnp.where(first, 0, 1))

    def tell(peer):
        pltpu.make_async_remote_copy(
            src_ref=told,
            dst_ref=heard.at[tm],
            send_sem=heard_ssem,
            recv_sem=heard_rsem,
            device_id=(sec, peer),
            device_id_type=MESH,
        ).start()

    def invite(peer):
        pl.semaphore_signal(ready, inc=1, device_id=(down, peer), device_id_type=MESH)

    pass_temb = pltpu.make_async_remote_copy(
        src_ref=temb,
        dst_ref=temb_next,
        send_sem=temb_ssem,
        recv_sem=temb_rsem,
        device_id=(down, tm),
        device_id_type=MESH,
    )

    @pl.when(first)
    def _():
        each(1, n_time, tell)

    for copy in small[1:4]:
        copy.wait()
    order = lax.broadcasted_iota(jnp.int32, (slots, half), 1).astype(jnp.float32)
    angles = steps_f * jnp.exp(-math.log(10000.0) * order / half)
    temb[...] = jnp.dot(
        jnp.sin(angles).astype(jnp.bfloat16), proj[0:half, :], preferred_element_type=jnp.float32
    ) + jnp.dot(
        jnp.cos(angles).astype(jnp.bfloat16), proj[half:chans, :], preferred_element_type=jnp.float32
    )

    @pl.when(jnp.logical_not(first))
    def _():
        each(0, n_time, invite)
        pass_temb.start()

    load_w(0).wait()

    @pl.when(deep)
    def _():
        for layer in range(1, layers):
            load_w(layer).wait()

    @pl.when(first)
    def _():
        columns = jnp.transpose(noisy[...])
        for m in range(micros):
            for f in range(rows_f):
                at = m * rows_f + f
                hmid[m, f * frames : (f + 1) * frames, :] = (
                    columns[:, at : at + 1] * lift[...] + temb[m : m + 1, :]
                )
        heard[tm] = told[...]
        for m in range(micros):
            for k in range(2 * halves):
                box[m, 0, :, edge_rows + k] = jnp.zeros_like(box[m, 0, :, edge_rows + k])
        if n_time > 1:
            others = heard.at[pl.ds(0, n_time - 1)]
            pltpu.make_async_copy(others, others, heard_rsem).wait()
        total = jnp.sum(heard[:, 0], axis=0)
        near = (heard[left, 2], heard[right, 1])
        for m in range(micros):
            shift = temb[m : m + 1, :]
            center = total[:, m : m + 1] / positions
            wide = jnp.maximum(
                total[:, micros + m : micros + m + 1] / positions - center * center, 0.0
            )
            middle = lift[...] * center + shift
            both = (
                positions * middle,
                positions * (lift[...] * lift[...] * wide + middle * middle),
            )
            for v in range(2):
                for k in range(halves):
                    box[m, 0, 0, edge_rows + v * halves + k] = both[v][
                        :, k * 128 : (k + 1) * 128
                    ]
            for side, peer in ((0, left), (1, right)):
                for f in range(rows_f):
                    at = m * rows_f + f
                    edge = near[side][:, at : at + 1] * lift[...] + shift
                    for k in range(halves):
                        box[m, 0, peer, k * rows_f + f] = edge[:, k * 128 : (k + 1) * 128]

    lax.fori_loop(0, 2 * micros, step, 0)

    @pl.when(first)
    def _():
        if n_time > 1:
            others = heard.at[pl.ds(0, n_time - 1)]
            pltpu.make_async_copy(others, others, heard_ssem).wait()

    @pl.when(jnp.logical_not(first))
    def _():
        pass_temb.wait_send()

    @pl.when(deep)
    def _():
        for m in range(micros):
            await_letters(let_ssem.at[m, 0], 0)

    @pl.when(jnp.logical_not(last))
    def _():
        for m in range(micros):
            await_letters(let_ssem.at[m, 1], 1)
            pltpu.make_async_copy(staged.at[m], staged.at[m], blk_ssem.at[m]).wait()


def on_device(clean, noise, timestep, lift, norm_gain, norm_bias, conv_weight, time_proj):
    n_time = lax.axis_size("tm")
    n_section = lax.axis_size("section")
    micros, rows_f, frames = clean.shape
    chans = lift.shape[0]
    layers = norm_gain.shape[1]
    slots = -(-micros // 8) * 8
    rows = rows_f * frames
    dims = (n_time, n_section, micros, rows_f, frames, chans, layers)
    letter_rows = (rows_f + 2) * (chans // 128)
    vmem = pl.BlockSpec(memory_space=pltpu.VMEM)
    hbm = pl.BlockSpec(memory_space=pl.ANY)
    dma = pltpu.SemaphoreType.DMA
    saved = pl.pallas_call(
        functools.partial(kernel, dims),
        out_shape=pltpu.VMEM((micros, rows, chans), jnp.bfloat16),
        in_specs=[hbm] * 8,
        out_specs=vmem,
        scratch_shapes=[
            pltpu.VMEM((layers, 3, 3 * chans, chans), jnp.bfloat16),
            pltpu.VMEM((micros, rows, chans), jnp.bfloat16),
            pltpu.VMEM((micros, rows, chans), jnp.float32),
            pltpu.VMEM((micros * rows_f, frames), jnp.float32),
            pltpu.VMEM((3, 1, 128), jnp.float32),
            pltpu.VMEM((n_time, 3, 1, 128), jnp.float32),
            pltpu.VMEM((slots, chans), jnp.float32),
            pltpu.VMEM((micros, rows_f, frames), jnp.float32),
            pltpu.VMEM((micros, rows_f, frames), jnp.float32),
            pltpu.VMEM((1, chans), jnp.float32),
            pltpu.VMEM((layers, chans), jnp.float32),
            pltpu.VMEM((layers, chans), jnp.float32),
            pltpu.VMEM((chans, chans), jnp.bfloat16),
            pltpu.VMEM((slots, chans), jnp.float32),
            pltpu.SMEM((micros,), jnp.int32),
            pltpu.VMEM((rows, 3 * chans), jnp.bfloat16),
            pltpu.VMEM((micros, 2, 2, letter_rows, 1, 128), jnp.float32),
            pltpu.VMEM((micros, 2, n_time, letter_rows, 1, 128), jnp.float32),
            pltpu.VMEM((2 * (chans // 128) * n_time + 2 * letter_rows, 1, 128), jnp.float32),
            dma((micros, 2)),
            dma((micros, 2)),
            dma((micros,)),
            dma((micros, 2)),
            dma((layers,)),
            dma((7,)),
            dma,
            dma,
            dma,
            dma,
            pltpu.SemaphoreType.REGULAR,
        ],
        compiler_params=pltpu.CompilerParams(
            collective_id=0, has_side_effects=True, vmem_limit_bytes=48 * 2**20
        ),
    )(
        *(
            pltpu.with_memory_space_constraint(x, pltpu.HBM)
            for x in (
                timestep,
                clean,
                noise,
                lift.reshape(1, chans),
                norm_gain,
                norm_bias,
                time_proj,
                conv_weight.reshape(layers, 3, 3 * chans, chans),
            )
        ),
    )
    return saved.reshape(1, micros, rows_f, frames, chans)


def solution(mesh):
    in_specs = (
        P(None, None, "tm"),
        P(None, None, "tm"),
        P(),
        P(),
        P("section", None, None),
        P("section", None, None),
        P("section", None, None, None, None, None),
        P("section", None, None),
    )
    out_specs = P("section", None, None, "tm", None)
    return jax.shard_map(
        on_device, mesh=mesh, in_specs=in_specs, out_specs=out_specs, check_vma=False
    )
```

```python
import functools
import math

import jax
import jax.numpy as jnp
from jax import lax
from jax.experimental import pallas as pl
from jax.experimental.pallas import tpu as pltpu
from jax.sharding import PartitionSpec as P

GROUPS = 32
STEPS = 1000
LEAD = 2
MIDDLE = 4
FIRST = 3
MESH = pl.DeviceIdType.MESH


def silu(half):
    return half + half * jnp.tanh(half)


def kernel(
    dims,
    steps_in,
    clean_in,
    noise_in,
    lift_in,
    gains_in,
    biases_in,
    proj_in,
    weights,
    staged,
    w,
    xin,
    hmid,
    noisy,
    told,
    heard,
    temb_next,
    clean,
    noise,
    lift,
    gains,
    biases,
    proj,
    temb,
    timestep,
    act3,
    letter,
    box,
    tally,
    let_ssem,
    let_rsem,
    blk_ssem,
    blk_rsem,
    w_sem,
    in_sem,
    heard_ssem,
    heard_rsem,
    temb_ssem,
    temb_rsem,
    ready,
):
    n_time, n_section, micros, rows_f, frames, chans, layers = dims
    rows = rows_f * frames
    positions = rows * n_time
    width = chans // GROUPS
    count = positions * width
    halves = chans // 128
    edge_rows = rows_f * halves
    sec = lax.axis_index("section")
    tm = lax.axis_index("tm")
    deep = sec < n_section // 2
    first = sec == 0
    last = sec == n_section - 1
    has_left = tm > 0
    has_right = tm < n_time - 1
    left = jnp.maximum(tm - 1, 0)
    right = jnp.minimum(tm + 1, n_time - 1)
    up = jnp.minimum(sec + 1, n_section - 1)
    down = jnp.maximum(sec - 1, 0)
    short = n_time <= 8

    def each(begin, end, one):
        def step(r, carry):
            one(lax.rem(tm + r, n_time))
            return carry

        lax.fori_loop(begin, end, step, 0, unroll=short)

    def load_w(layer):
        return pltpu.make_async_copy(weights.at[layer], w.at[layer], w_sem.at[layer])

    small = [
        pltpu.make_async_copy(src, dst, in_sem.at[k])
        for k, (src, dst) in enumerate(
            [
                (steps_in, timestep),
                (proj_in.at[0], proj),
                (gains_in.at[0], gains),
                (biases_in.at[0], biases),
                (clean_in, clean),
                (noise_in, noise),
                (lift_in, lift),
            ]
        )
    ]

    barrier = pltpu.get_barrier_semaphore()

    def greet(section):
        def one(peer):
            pl.semaphore_signal(
                barrier, inc=1, device_id=(section, peer), device_id_type=MESH
            )

        return one

    each(1, n_time, greet(sec))

    small[0].start()

    @pl.when(first)
    def _():
        for copy in small[4:]:
            copy.start()

    for copy in small[1:4]:
        copy.start()

    @pl.when(jnp.logical_not(last))
    def _():
        each(0, n_time, greet(up))

    load_w(0).start()

    @pl.when(deep)
    def _():
        for layer in range(1, layers):
            load_w(layer).start()

    lanes = lax.broadcasted_iota(jnp.int32, (8, 128), 1)
    tiers = lax.broadcasted_iota(jnp.int32, (8, 128), 0)
    spot = lanes % width
    quad = lanes % 4

    def turn(value, step):
        return value if step == 0 else pltpu.roll(value, step % 128, 1)

    def group_total(tall):
        total = tall
        for r in range(1, width):
            total = total + jnp.where(spot < width - r, turn(tall, -r), turn(tall, width - r))
        return total

    def pack(s1, s2):
        tall = jnp.where(
            tiers < 2,
            jnp.where(tiers == 0, s1[:, 0:128], s1[:, 128:256]),
            jnp.where(tiers == 2, s2[:, 0:128], s2[:, 128:256]),
        )
        total = group_total(tall)
        return jnp.sum(jnp.where(tiers == quad, total, 0.0), axis=0, keepdims=True)

    def spread(stats):
        tall = jnp.where(
            tiers < 2,
            jnp.where(tiers == 0, stats[0], stats[1]),
            jnp.where(tiers == 2, stats[2], stats[3]),
        )
        total = group_total(tall)
        return [total[k : k + 1] for k in range(2 * halves)]

    def unpack(packed):
        wide = jnp.broadcast_to(packed, (8, 128))
        turned = {k: turn(wide, k) for k in range(-3, 4)}
        found = []
        for v in range(4):
            low = jnp.where(quad == 0, turned[-v], turned[1 - v])
            high = jnp.where(quad == 2, turned[2 - v], turned[3 - v])
            found.append(jnp.where(quad < 2, low, high)[0:1])
        return found

    def summarize(m, kind, value):
        s1 = jnp.sum(value, axis=0, keepdims=True)
        s2 = jnp.sum(value * value, axis=0, keepdims=True)
        if kind:
            stats = [pack(s1, s2)]
        else:
            stats = [v[:, k * 128 : (k + 1) * 128] for v in (s1, s2) for k in range(halves)]
        for side in range(2):
            for f in range(rows_f):
                at = f * frames + side * (frames - 1)
                for k in range(halves):
                    letter[m, kind, side, k * rows_f + f] = value[
                        at : at + 1, k * 128 : (k + 1) * 128
                    ]
            for k, stat in enumerate(stats):
                letter[m, kind, side, edge_rows + k] = stat

    def post(m, kind, side, begin, rows_sent, section, peer):
        pltpu.make_async_remote_copy(
            src_ref=letter.at[m, kind, side, pl.ds(begin, rows_sent)],
            dst_ref=box.at[m, 1 - kind, tm, pl.ds(begin, rows_sent)],
            send_sem=let_ssem.at[m, kind],
            recv_sem=let_rsem.at[m, 1 - kind],
            device_id=(section, peer),
            device_id_type=MESH,
        ).start()

    stat_rows = (2 * halves, 1)

    def publish(m, kind, section, between=None):
        span = stat_rows[kind]

        def plain(peer):
            post(m, kind, 0, edge_rows, span, section, peer)

        @pl.when(has_right)
        def _():
            post(m, kind, 1, 0, edge_rows + span, section, right)

        @pl.when(has_left)
        def _():
            post(m, kind, 0, 0, edge_rows + span, section, left)

        if n_time > 2:

            @pl.when(jnp.logical_not(has_right))
            def _():
                plain(0)

            @pl.when(jnp.logical_not(has_left))
            def _():
                plain(n_time - 1)

        each(2, max(n_time // 2, 2), plain)
        if between is not None:
            between()
        each(max(n_time // 2, 2), n_time - 1, plain)

        if kind:
            plain(tm)
        else:
            for k in range(span):
                box[m, 1, tm, edge_rows + k] = letter[m, 0, 0, edge_rows + k]

    def await_letters(sem, kind):
        plain = (n_time if kind else n_time - 1) * stat_rows[kind]

        def take(long):
            whole = tally.at[pl.ds(0, plain + long * edge_rows)]
            pltpu.make_async_copy(whole, whole, sem).wait()

        if n_time > 2:
            both = jnp.logical_and(has_left, has_right)

            @pl.when(both)
            def _():
                take(2)

            @pl.when(jnp.logical_not(both))
            def _():
                take(1)

        elif n_time == 2:
            take(1)
        elif plain:
            take(0)

    def convolve(m, layer, stats, stages, load):
        low1, high1, low2, high2 = stats
        gain = gains[pl.ds(layer, 1), :]
        bias = biases[pl.ds(layer, 1), :]
        scales, offsets = [], []
        for k, (s1, s2) in enumerate([(low1, low2), (high1, high2)]):
            at = slice(k * 128, (k + 1) * 128)
            mean = s1 / count
            var = jnp.maximum(s2 / count - mean * mean, 0.0)
            scale = lax.rsqrt(var + 1e-05) * (0.5 * gain[:, at])
            scales.append(scale)
            offsets.append(0.5 * bias[:, at] - mean * scale)
        scale = jnp.concatenate(scales, axis=1)
        offset = jnp.concatenate(offsets, axis=1)
        beyond = []
        for near, there in ((left, has_left), (right, has_right)):
            tall = jnp.concatenate([box[m, layer, near, r] for r in range(edge_rows)], axis=0)
            parts = [
                silu(tall[k * rows_f : (k + 1) * rows_f] * scales[k] + offsets[k])
                for k in range(halves)
            ]
            beyond.append(jnp.where(there, jnp.concatenate(parts, axis=1), 0.0))
        before, after = beyond
        place = lax.broadcasted_iota(jnp.int32, (frames, chans), 0)
        sums = [None] * rows_f

        def add(f, value):
            sums[f] = value if sums[f] is None else sums[f] + value

        for low, high, taps in stages:
            hidden = load(low, high)
            act = silu(hidden * scale + offset)
            for f in range(low, high):
                at = slice((f - low) * frames, (f - low + 1) * frames)
                add(f, hidden[at])
                row = act[at]
                prev = jnp.where(place == 0, before[f : f + 1], pltpu.roll(row, 1, 0))
                nxt = jnp.where(
                    place == frames - 1, after[f : f + 1], pltpu.roll(row, frames - 1, 0)
                )
                at = slice(f * frames, (f + 1) * frames)
                act3[at, 0:chans] = prev.astype(jnp.bfloat16)
                act3[at, chans : 2 * chans] = row.astype(jnp.bfloat16)
                act3[at, 2 * chans : 3 * chans] = nxt.astype(jnp.bfloat16)
            for i in taps:
                used = [f for f in range(rows_f) if 0 <= f - i + 1 < rows_f]
                span = slice(used[0] * frames, (used[-1] + 1) * frames)
                product = jnp.dot(act3[span], w[layer, i], preferred_element_type=jnp.float32)
                for k, f in enumerate(used):
                    add(f - i + 1, product[k * frames : (k + 1) * frames])
        hidden = jnp.concatenate(sums, axis=0)
        hmid[m] = hidden
        staged[m] = hidden.astype(jnp.bfloat16)

    def block_copy(m, begin, end, piece):
        span = pl.ds(begin, end - begin)
        return pltpu.make_async_remote_copy(
            src_ref=staged.at[m, span],
            dst_ref=xin.at[m, span],
            send_sem=blk_ssem.at[m],
            recv_sem=blk_rsem.at[m, piece],
            device_id=(up, tm),
            device_id_type=MESH,
        )

    ahead = jnp.where(first, min(FIRST, micros), min(2, micros))

    def step(k, carry):
        past = jnp.maximum(k - ahead, 0)
        rest = micros - ahead
        filling = k < ahead
        mixing = past < 2 * rest
        odd = lax.rem(past, 2) == 1
        entering = jnp.logical_or(filling, jnp.logical_and(mixing, odd))
        m = jnp.where(mixing, jnp.where(odd, ahead + past // 2, past // 2), past - rest)
        m = jnp.where(filling, k, m)
        landing = jnp.logical_and(entering, jnp.logical_not(first))
        stay = jnp.logical_and(entering, deep)
        rises = jnp.logical_not(jnp.logical_or(stay, last))
        layer = jnp.where(entering, 0, 1)

        @pl.when(landing)
        def _():
            await_letters(let_rsem.at[m, 0], 1)
            stats = unpack(jnp.sum(box[m, 0, :, edge_rows], axis=0))

            def load(low, high):
                landed = xin.at[m, pl.ds(low * frames, (high - low) * frames)]
                pltpu.make_async_copy(landed, landed, blk_rsem.at[m, 1 if low else 0]).wait()
                span = slice(low * frames, high * frames)
                return xin[m, span, :].astype(jnp.float32) + temb[pl.ds(m, 1), :]

            convolve(m, layer, stats, ((0, rows_f - 1, (0,)), (rows_f - 1, rows_f, (1, 2))), load)

        @pl.when(jnp.logical_or(stay, deep) & jnp.logical_not(landing))
        def _():
            @pl.when(jnp.logical_not(entering))
            def _():
                await_letters(let_rsem.at[m, 1], 0)

            stats = spread(
                [
                    jnp.sum(box[m, layer, :, edge_rows + k], axis=0)
                    for k in range(2 * halves)
                ]
            )
            convolve(
                m,
                layer,
                stats,
                ((0, rows_f, (0, 1, 2)),),
                lambda low, high: hmid[m, low * frames : high * frames, :],
            )

        @pl.when(stay)
        def _():
            summarize(m, 0, hmid[m])
            publish(m, 0, sec)

        @pl.when(jnp.logical_and(jnp.logical_or(entering, deep), rises))
        def _():
            @pl.when(m == 0)
            def _():
                pl.semaphore_wait(ready, n_time)
                pltpu.make_async_copy(temb_next, temb_next, temb_rsem).wait()

            block_copy(m, 0, LEAD * frames // 4, 0).start()
            summarize(m, 1, staged[m].astype(jnp.float32) + temb_next[pl.ds(m, 1), :])
            publish(
                m,
                1,
                up,
                lambda: block_copy(m, LEAD * frames // 4, MIDDLE * frames // 4, 0).start(),
            )
            block_copy(m, MIDDLE * frames // 4, (rows_f - 1) * frames, 0).start()
            block_copy(m, (rows_f - 1) * frames, rows, 1).start()

        return carry

    small[0].wait()
    half = chans // 2
    slots = temb.shape[0]
    which = lax.broadcasted_iota(jnp.int32, (slots, half), 0)
    steps_f = jnp.zeros((slots, half), jnp.float32)
    for m in range(micros):
        steps_f = jnp.where(which == m, timestep[m].astype(jnp.float32), steps_f)

    @pl.when(first)
    def _():
        level = jnp.cos(math.pi / 2.0 * (steps_f / STEPS + 0.008) / 1.008) ** 2
        keep = jnp.sqrt(level)
        blur = jnp.sqrt(1.0 - level)
        for copy in small[4:]:
            copy.wait()
        lane = lax.broadcasted_iota(jnp.int32, (1, 128), 1)
        tallies = jnp.zeros((1, 128), jnp.float32)
        for m in range(micros):
            mixed = keep[m : m + 1, 0:1] * clean[m] + blur[m : m + 1, 0:1] * noise[m]
            noisy[m * rows_f : (m + 1) * rows_f, :] = mixed
            for k, value in enumerate((mixed, mixed * mixed)):
                flat = jnp.sum(jnp.sum(value, axis=0, keepdims=True), axis=1, keepdims=True)
                tallies = jnp.where(lane == k * micros + m, flat, tallies)
        told[0] = tallies
        columns = jnp.transpose(noisy[...])
        told[1, :, 0 : micros * rows_f] = columns[0:1, :]
        told[2, :, 0 : micros * rows_f] = columns[frames - 1 : frames, :]

    pl.semaphore_wait(barrier, n_time - 1 + n_time * jnp.where(first, 0, 1))

    def tell(peer):
        pltpu.make_async_remote_copy(
            src_ref=told,
            dst_ref=heard.at[tm],
            send_sem=heard_ssem,
            recv_sem=heard_rsem,
            device_id=(sec, peer),
            device_id_type=MESH,
        ).start()

    def invite(peer):
        pl.semaphore_signal(ready, inc=1, device_id=(down, peer), device_id_type=MESH)

    pass_temb = pltpu.make_async_remote_copy(
        src_ref=temb,
        dst_ref=temb_next,
        send_sem=temb_ssem,
        recv_sem=temb_rsem,
        device_id=(down, tm),
        device_id_type=MESH,
    )

    @pl.when(first)
    def _():
        each(1, n_time, tell)

    for copy in small[1:4]:
        copy.wait()
    order = lax.broadcasted_iota(jnp.int32, (slots, half), 1).astype(jnp.float32)
    angles = steps_f * jnp.exp(-math.log(10000.0) * order / half)
    temb[...] = jnp.dot(
        jnp.sin(angles).astype(jnp.bfloat16), proj[0:half, :], preferred_element_type=jnp.float32
    ) + jnp.dot(
        jnp.cos(angles).astype(jnp.bfloat16), proj[half:chans, :], preferred_element_type=jnp.float32
    )

    @pl.when(jnp.logical_not(first))
    def _():
        each(0, n_time, invite)
        pass_temb.start()

    load_w(0).wait()

    @pl.when(deep)
    def _():
        for layer in range(1, layers):
            load_w(layer).wait()

    @pl.when(first)
    def _():
        columns = jnp.transpose(noisy[...])
        for m in range(micros):
            for f in range(rows_f):
                at = m * rows_f + f
                hmid[m, f * frames : (f + 1) * frames, :] = (
                    columns[:, at : at + 1] * lift[...] + temb[m : m + 1, :]
                )
        heard[tm] = told[...]
        for m in range(micros):
            for k in range(2 * halves):
                box[m, 0, :, edge_rows + k] = jnp.zeros_like(box[m, 0, :, edge_rows + k])
        if n_time > 1:
            others = heard.at[pl.ds(0, n_time - 1)]
            pltpu.make_async_copy(others, others, heard_rsem).wait()
        total = jnp.sum(heard[:, 0], axis=0)
        near = (heard[left, 2], heard[right, 1])
        for m in range(micros):
            shift = temb[m : m + 1, :]
            center = total[:, m : m + 1] / positions
            wide = jnp.maximum(
                total[:, micros + m : micros + m + 1] / positions - center * center, 0.0
            )
            middle = lift[...] * center + shift
            both = (
                positions * middle,
                positions * (lift[...] * lift[...] * wide + middle * middle),
            )
            for v in range(2):
                for k in range(halves):
                    box[m, 0, 0, edge_rows + v * halves + k] = both[v][
                        :, k * 128 : (k + 1) * 128
                    ]
            for side, peer in ((0, left), (1, right)):
                for f in range(rows_f):
                    at = m * rows_f + f
                    edge = near[side][:, at : at + 1] * lift[...] + shift
                    for k in range(halves):
                        box[m, 0, peer, k * rows_f + f] = edge[:, k * 128 : (k + 1) * 128]

    lax.fori_loop(0, 2 * micros, step, 0)

    @pl.when(first)
    def _():
        if n_time > 1:
            others = heard.at[pl.ds(0, n_time - 1)]
            pltpu.make_async_copy(others, others, heard_ssem).wait()

    @pl.when(jnp.logical_not(first))
    def _():
        pass_temb.wait_send()

    @pl.when(deep)
    def _():
        for m in range(micros):
            await_letters(let_ssem.at[m, 0], 0)

    @pl.when(jnp.logical_not(last))
    def _():
        for m in range(micros):
            await_letters(let_ssem.at[m, 1], 1)
            pltpu.make_async_copy(staged.at[m], staged.at[m], blk_ssem.at[m]).wait()


def on_device(clean, noise, timestep, lift, norm_gain, norm_bias, conv_weight, time_proj):
    n_time = lax.axis_size("tm")
    n_section = lax.axis_size("section")
    micros, rows_f, frames = clean.shape
    chans = lift.shape[0]
    layers = norm_gain.shape[1]
    slots = -(-micros // 8) * 8
    rows = rows_f * frames
    dims = (n_time, n_section, micros, rows_f, frames, chans, layers)
    letter_rows = (rows_f + 2) * (chans // 128)
    vmem = pl.BlockSpec(memory_space=pltpu.VMEM)
    hbm = pl.BlockSpec(memory_space=pl.ANY)
    dma = pltpu.SemaphoreType.DMA
    saved = pl.pallas_call(
        functools.partial(kernel, dims),
        out_shape=pltpu.VMEM((micros, rows, chans), jnp.bfloat16),
        in_specs=[hbm] * 8,
        out_specs=vmem,
        scratch_shapes=[
            pltpu.VMEM((layers, 3, 3 * chans, chans), jnp.bfloat16),
            pltpu.VMEM((micros, rows, chans), jnp.bfloat16),
            pltpu.VMEM((micros, rows, chans), jnp.float32),
            pltpu.VMEM((micros * rows_f, frames), jnp.float32),
            pltpu.VMEM((3, 1, 128), jnp.float32),
            pltpu.VMEM((n_time, 3, 1, 128), jnp.float32),
            pltpu.VMEM((slots, chans), jnp.float32),
            pltpu.VMEM((micros, rows_f, frames), jnp.float32),
            pltpu.VMEM((micros, rows_f, frames), jnp.float32),
            pltpu.VMEM((1, chans), jnp.float32),
            pltpu.VMEM((layers, chans), jnp.float32),
            pltpu.VMEM((layers, chans), jnp.float32),
            pltpu.VMEM((chans, chans), jnp.bfloat16),
            pltpu.VMEM((slots, chans), jnp.float32),
            pltpu.SMEM((micros,), jnp.int32),
            pltpu.VMEM((rows, 3 * chans), jnp.bfloat16),
            pltpu.VMEM((micros, 2, 2, letter_rows, 1, 128), jnp.float32),
            pltpu.VMEM((micros, 2, n_time, letter_rows, 1, 128), jnp.float32),
            pltpu.VMEM((2 * (chans // 128) * n_time + 2 * letter_rows, 1, 128), jnp.float32),
            dma((micros, 2)),
            dma((micros, 2)),
            dma((micros,)),
            dma((micros, 2)),
            dma((layers,)),
            dma((7,)),
            dma,
            dma,
            dma,
            dma,
            pltpu.SemaphoreType.REGULAR,
        ],
        compiler_params=pltpu.CompilerParams(
            collective_id=0, has_side_effects=True, vmem_limit_bytes=48 * 2**20
        ),
    )(
        *(
            pltpu.with_memory_space_constraint(x, pltpu.HBM)
            for x in (
                timestep,
                clean,
                noise,
                lift.reshape(1, chans),
                norm_gain,
                norm_bias,
                time_proj,
                conv_weight.reshape(layers, 3, 3 * chans, chans),
            )
        ),
    )
    return saved.reshape(1, micros, rows_f, frames, chans)


def solution(mesh):
    in_specs = (
        P(None, None, "tm"),
        P(None, None, "tm"),
        P(),
        P(),
        P("section", None, None),
        P("section", None, None),
        P("section", None, None, None, None, None),
        P("section", None, None),
    )
    out_specs = P("section", None, None, "tm", None)
    return jax.shard_map(
        on_device, mesh=mesh, in_specs=in_specs, out_specs=out_specs, check_vma=False
    )
```
